32 devices in a mesh: pass: 2 (over y), az: 8 (over z, x), rg: 2 (over core).
Axes of the slice: x: 2, y: 2, z: 4, core: 2. Of those that a mesh axis runs over, the one named last changes fastest.
Arguments:
- reference_slc: bfloat16 [2, 4096, 10240], P(None, ('pass', 'az'), 'rg'), parts along dimension 1, may hold values from -8 to 8, as said below
- secondary_slc: bfloat16 [2, 4096, 10240], P(None, ('pass', 'az'), 'rg'), parts along dimension 1, may hold values from -20 to 20, as said below
- line_target: int32 [1024], P(('pass', 'az')), parts along dimension 0, may hold values from 0 to 511, as said below
- seam_partner: int32 [1024], P(('pass', 'az')), parts along dimension 0, may hold values from -1 to 63, as said below
- mask_level: int32 [1024, 512], P(('pass', 'az'), 'rg'), parts along dimension 0, may hold values from 0 to 3
Outputs:
- unwrapped: float32 [1024, 512], P(('pass', 'az'), 'rg'), parts along dimension 0
- residual: float32 [1024, 512], P(('pass', 'az'), 'rg'), parts along dimension 0
The draws below stay inside these ranges and needn't reach their ends.
There are 2 independent parts, one for each index of `pass`. The reference program is written for one: setup_inputs(seed, part) draws one part's arguments, and reference() takes and returns one part's arrays. A program takes and returns all parts, laid end to end along the dimension named above; each array names one. Nothing has to cross between parts.
Inputs may be any that keep to these rules, and one draw needn't show every extreme that they name: `reference_slc`: real and imaginary planes of complex samples. `secondary_slc`: real and imaginary planes of complex samples. `line_target`: A permutation of the 512 grid rows, indexed by look row in acquisition order. Every owner of 64 grid rows receives exactly 64 look rows; no owner receives more than 16 look rows from one device, and every device sends exactly 16 look rows to at least one owner. `seam_partner`: -1 where a grid row has no partner, else the index within the next block of 64 grid rows of the row that images the same ground; the partners within a block are distinct, and the last 64 rows have none.
All inputs are finite; a program needn't handle non-finite values.
Results may differ from the reference program's by a relative error of at most 0.0003.
Values sent between devices are 32-bit elements; how exact they have to be, the bound alone decides.
A program may use at most 192 MiB of HBM per device.

```python
import math
import jax
import jax.numpy as jnp
from jax import lax

LOOK_AZ = 4
LOOK_RG = 20
R_DEV = 64
ITERS = 2
ROWS = 512
COLS = 512
N_AZ = 8


def slc_pair(key):
    line_total = LOOK_AZ * ROWS
    sample_total = LOOK_RG * COLS
    base_key = jax.random.fold_in(key, 4101)
    ref_key, phase_key, noise_key = jax.random.split(base_key, 3)
    shape_full = (2, line_total, sample_total)
    ref_planes = jnp.clip(jax.random.normal(ref_key, shape_full, jnp.float32), -6.0, 6.0)
    noise_planes = jnp.clip(jax.random.normal(noise_key, shape_full, jnp.float32), -6.0, 6.0)
    phase_cells = jax.random.uniform(phase_key, (ROWS, COLS), jnp.float32, -math.pi, math.pi)
    phase_full = jnp.repeat(jnp.repeat(phase_cells, LOOK_AZ, axis=0), LOOK_RG, axis=1)
    spread = 0.2 + 1.5 * jnp.arange(line_total, dtype=jnp.float32)[:, None] / line_total
    cosine = jnp.cos(phase_full)
    sine = jnp.sin(phase_full)
    sec_real = cosine * ref_planes[0] - sine * ref_planes[1] + spread * noise_planes[0]
    sec_imag = sine * ref_planes[0] + cosine * ref_planes[1] + spread * noise_planes[1]
    return (ref_planes, jnp.stack([sec_real, sec_imag]))


def draw_reference_slc(key, part):
    return slc_pair(key)[0].astype(jnp.bfloat16)


def draw_secondary_slc(key, part):
    return slc_pair(key)[1].astype(jnp.bfloat16)


def draw_line_target(key, part):
    device_total = N_AZ
    row_total = R_DEV
    capacity = max(2, 2 * row_total // device_total)
    size_key, offset_key, order_key = jax.random.split(jax.random.fold_in(key, 733), 3)
    group_sizes = jax.random.randint(size_key, (device_total,), capacity // 2, capacity + 1)
    group_sizes = group_sizes.at[0].set(capacity)
    group_ends = jnp.minimum(jnp.cumsum(group_sizes), row_total)
    offsets = jax.random.permutation(offset_key, device_total)
    slot_of = jax.vmap(lambda b: jax.random.permutation(jax.random.fold_in(order_key, b), row_total))(jnp.arange(device_total))
    group_of = jnp.sum((group_ends[None, None, :] <= slot_of[:, :, None]).astype(jnp.int32), axis=2)
    owner_dev = (jnp.arange(device_total)[:, None] + offsets[group_of]) % device_total
    return (owner_dev * row_total + slot_of).reshape(-1).astype(jnp.int32)


def draw_seam_partner(key, part):
    device_total = N_AZ
    row_total = R_DEV
    count_key, match_key = jax.random.split(jax.random.fold_in(key, 977))
    seam_count = jax.random.randint(count_key, (device_total,), row_total // 4, row_total // 2 + 1)
    matches = jax.vmap(lambda b: jax.random.permutation(jax.random.fold_in(match_key, b), row_total))(jnp.arange(device_total))
    local_row = jnp.arange(row_total)
    position = local_row[None, :] - (row_total - seam_count[:, None])
    chosen = jnp.take_along_axis(matches, jnp.clip(position, 0, row_total - 1), axis=1)
    linked = (position >= 0) & (jnp.arange(device_total)[:, None] < device_total - 1)
    return jnp.where(linked, chosen, -1).reshape(-1).astype(jnp.int32)


def set_ends(values, rng, low, high):
    longest = values.shape.index(max(values.shape))
    spots = []
    for shift in (0, 1):
        where = [jax.random.randint(jax.random.fold_in(rng, axis), (), 0, length) for axis, length in enumerate(values.shape)]
        where[longest] = (where[longest] + shift) % values.shape[longest]
        spots.append(tuple(where))
    return values.at[spots[0]].set(low).at[spots[1]].set(high)


def setup_inputs(seed: int = 0, part: int = 0) -> dict:
    key_list = jax.random.split(jax.random.key(seed), 6)
    own_keys = jax.random.split(jax.random.fold_in(key_list[5], part), 6)
    reference_slc = draw_reference_slc(jax.random.fold_in(jax.random.fold_in(key_list[5], part), 71), part)
    secondary_slc = draw_secondary_slc(jax.random.fold_in(jax.random.fold_in(key_list[5], part), 71), part)
    line_target = draw_line_target(jax.random.fold_in(jax.random.fold_in(key_list[5], part), 71), part)
    seam_partner = draw_seam_partner(jax.random.fold_in(jax.random.fold_in(key_list[5], part), 71), part)
    mask_level = set_ends(jax.random.randint(own_keys[4], (ROWS, COLS), 0, 4), jax.random.fold_in(own_keys[4], 1), 0, 3).astype(jnp.int32)
    return dict(reference_slc=reference_slc, secondary_slc=secondary_slc, line_target=line_target, seam_partner=seam_partner, mask_level=mask_level)


FULL_PRECISION = lax.Precision.HIGHEST
EPSILON = 1e-06

def dct_table(freq_index, place_index, length):
    product = (2 * place_index[None, :] + 1) * freq_index[:, None] % (4 * length)
    norm_factor = jnp.where(freq_index == 0, math.sqrt(1.0 / length), math.sqrt(2.0 / length)).astype(jnp.float32)
    return norm_factor[:, None] * jnp.cos(product.astype(jnp.float32) * (math.pi / (2.0 * length)))

def eigenvalues(freq_index, length):
    return 4.0 * jnp.sin(freq_index.astype(jnp.float32) * (math.pi / (2.0 * length))) ** 2

def neighbours(padded):
    return (padded[..., :-2, 1:-1], padded[..., 2:, 1:-1], padded[..., 1:-1, :-2], padded[..., 1:-1, 2:])

def matmul(left, right):
    return jnp.dot(left, right, precision=FULL_PRECISION, preferred_element_type=jnp.float32)

def reference(reference_slc, secondary_slc, line_target, seam_partner, mask_level):
    ref_real = reference_slc[0].astype(jnp.float32)
    ref_imag = reference_slc[1].astype(jnp.float32)
    sec_real = secondary_slc[0].astype(jnp.float32)
    sec_imag = secondary_slc[1].astype(jnp.float32)
    planes = jnp.stack([ref_real * sec_real + ref_imag * sec_imag, ref_imag * sec_real - ref_real * sec_imag, ref_real * ref_real + ref_imag * ref_imag, sec_real * sec_real + sec_imag * sec_imag])
    look_stack = planes.reshape(4, ROWS, LOOK_AZ, COLS, LOOK_RG).sum(axis=(2, 4))
    gridded = jnp.zeros((4, ROWS, COLS), jnp.float32).at[:, line_target].set(look_stack)
    row_index = jnp.arange(ROWS, dtype=jnp.int32)
    partner_row = jnp.minimum((row_index // R_DEV + 1) * R_DEV + jnp.maximum(seam_partner, 0), ROWS - 1).astype(jnp.int32)
    combined = gridded + jnp.where((seam_partner >= 0)[None, :, None], gridded[:, partner_row], 0.0)
    magnitude = jnp.sqrt(combined[2] * combined[3]) + EPSILON
    weight = (1 + mask_level).astype(jnp.float32) * 0.25
    fields = jnp.stack([combined[0] / magnitude, combined[1] / magnitude, weight])
    padded = jnp.pad(fields, ((0, 0), (1, 1), (1, 1)))
    beside_all = neighbours(padded)
    edge_weights = [weight * item[2] for item in beside_all]
    right_side = jnp.zeros((ROWS, COLS), jnp.float32)
    for edge, item in zip(edge_weights, beside_all):
        right_side = right_side + edge * (fields[1] * item[0] - fields[0] * item[1])
    damping = 0.25 / (R_DEV * R_DEV)

    def apply_operator(values):
        rim = jnp.pad(values, 1)
        result_sum = damping * values
        for edge, item in zip(edge_weights, neighbours(rim)):
            result_sum = result_sum + edge * (values - item)
        return result_sum
    row_freq = jnp.arange(ROWS, dtype=jnp.int32)
    col_freq = jnp.arange(COLS, dtype=jnp.int32)
    row_basis = dct_table(row_freq, row_freq, ROWS)
    col_basis = dct_table(col_freq, col_freq, COLS)
    divisor = eigenvalues(row_freq, ROWS)[:, None] + eigenvalues(col_freq, COLS)[None, :] + damping

    def precondition(values):
        spectrum = matmul(matmul(row_basis, values), col_basis.T) / divisor
        return matmul(matmul(row_basis.T, spectrum), col_basis)
    solution = jnp.zeros((ROWS, COLS), jnp.float32)
    residual = right_side
    precond = precondition(residual)
    direction = precond
    inner_now = jnp.sum(residual * precond)
    for turn_index in range(ITERS):
        image_now = apply_operator(direction)
        step_size = inner_now / jnp.sum(direction * image_now)
        solution = solution + step_size * direction
        residual = residual - step_size * image_now
        if turn_index + 1 < ITERS:
            precond = precondition(residual)
            inner_next = jnp.sum(residual * precond)
            direction = precond + inner_next / inner_now * direction
            inner_now = inner_next
    return (solution, residual)
```

```python
import functools
import math

import jax
import jax.numpy as jnp
import numpy as np
from jax import lax
from jax.experimental import pallas as pl
from jax.experimental.pallas import tpu as pltpu
from jax.sharding import PartitionSpec as P

LOOK_AZ = 4
LOOK_RG = 20
ITERS = 2


FULL_PRECISION = lax.Precision.HIGHEST
EPSILON = 1e-06


def from_behind(value, axis, steps):
    count = lax.axis_size(axis)
    first, last = (max(0, -steps), min(count, count - steps))
    return lax.ppermute(value, axis, [(source, source + steps) for source in range(first, last)])


def with_halo(shard, sides, width):
    for axis, dim in sides:
        peers, length = (lax.axis_size(axis), shard.shape[dim])
        up = [(i, (i + 1) % peers) for i in range(peers - 1)]
        down = [(j, i) for i, j in up]
        last = lax.slice_in_dim(shard, length - width, length, axis=dim)
        first = lax.slice_in_dim(shard, 0, width, axis=dim)
        before = lax.ppermute(last, axis, up)
        after = lax.ppermute(first, axis, down)
        shard = jnp.concatenate([before, shard, after], axis=dim)
    return shard


def dct_table(freq_index, place_index, length):
    product = (2 * place_index[None, :] + 1) * freq_index[:, None] % (4 * length)
    norm_factor = jnp.where(
        freq_index == 0, math.sqrt(1.0 / length), math.sqrt(2.0 / length)
    ).astype(jnp.float32)
    return norm_factor[:, None] * jnp.cos(product.astype(jnp.float32) * (math.pi / (2.0 * length)))


def eigenvalues(freq_index, length):
    return 4.0 * jnp.sin(freq_index.astype(jnp.float32) * (math.pi / (2.0 * length))) ** 2


def neighbours(padded):
    return (
        padded[..., :-2, 1:-1],
        padded[..., 2:, 1:-1],
        padded[..., 1:-1, :-2],
        padded[..., 1:-1, 2:],
    )


def contract(left, right, left_dim, right_dim):
    return lax.dot_general(
        left,
        right,
        (((left_dim,), (right_dim,)), ((), ())),
        precision=FULL_PRECISION,
        preferred_element_type=jnp.float32,
    )


CHUNK = 256


def look_kernel(lines, half, ref_ref, sec_ref, group_ref, line_ref, out_ref):
    step_rows = lines // LOOK_AZ
    width = half // LOOK_RG
    for side in range(out_ref.shape[2] // width):
        total = jnp.zeros((8 * lines, width), jnp.float32)
        for start in range(0, half, CHUNK):
            span = pl.ds(side * half + start, CHUNK)
            mr = ref_ref[0, :, span].astype(jnp.float32)
            mi = ref_ref[1, :, span].astype(jnp.float32)
            sr = sec_ref[0, :, span].astype(jnp.float32)
            si = sec_ref[1, :, span].astype(jnp.float32)
            planes = jnp.concatenate(
                [mr * sr + mi * si, mi * sr - mr * si, mr * mr + mi * mi, sr * sr + si * si], axis=0
            )
            high = planes.astype(jnp.bfloat16)
            low = (planes - high.astype(jnp.float32)).astype(jnp.bfloat16)
            total = total + jnp.dot(
                jnp.concatenate([high, low], axis=0),
                group_ref[pl.ds(start, CHUNK), :],
                preferred_element_type=jnp.float32,
            )
        joined = total[: 4 * lines] + total[4 * lines :]
        sums = jnp.dot(
            line_ref[...], joined, precision=FULL_PRECISION, preferred_element_type=jnp.float32
        )
        for plane in range(4):
            out_ref[plane, :, side * width : (side + 1) * width] = sums[
                plane * step_rows : (plane + 1) * step_rows
            ]


def form_looks(ref_lines, sec_lines, col_count):
    line_count, sample_count = ref_lines.shape[1:]
    lines = 32
    half = 128 * LOOK_RG
    group = (np.arange(half)[:, None] // LOOK_RG == np.arange(128)[None, :]).astype(jnp.bfloat16)
    line_of = (np.arange(4 * lines)[None, :] // LOOK_AZ == np.arange(lines)[:, None]).astype(
        np.float32
    )
    block = pl.BlockSpec((2, lines, sample_count), lambda i: (0, i, 0))
    return pl.pallas_call(
        functools.partial(look_kernel, lines, half),
        grid=(line_count // lines,),
        in_specs=[
            block,
            block,
            pl.BlockSpec(group.shape, lambda i: (0, 0)),
            pl.BlockSpec(line_of.shape, lambda i: (0, 0)),
        ],
        out_specs=pl.BlockSpec((4, lines // LOOK_AZ, col_count), lambda i: (0, i, 0)),
        out_shape=jax.ShapeDtypeStruct((4, line_count // LOOK_AZ, col_count), jnp.float32),
        name="form_looks",
    )(ref_lines, sec_lines, group, line_of)


def iota(shape, dim):
    return lax.broadcasted_iota(jnp.int32, shape, dim)


def split(values):
    high = values.astype(jnp.bfloat16)
    rest = values - high.astype(jnp.float32)
    middle = rest.astype(jnp.bfloat16)
    return high, middle, (rest - middle.astype(jnp.float32)).astype(jnp.bfloat16)


def narrow_dot(left, right):
    return jnp.dot(left, right, preferred_element_type=jnp.float32)


def pick_dot(choose_thrice, values):
    return narrow_dot(choose_thrice, jnp.concatenate(split(values), axis=0))


def left_dot(parts, values):
    high, middle, low = split(values)
    return narrow_dot(parts, jnp.concatenate([low, middle, high, middle, high, high], axis=0))


def basis_dot(values, basis):
    count = values.shape[0]
    high, middle, low = split(values)
    first = narrow_dot(jnp.concatenate([high, middle, low], axis=0), basis[0])
    second = narrow_dot(jnp.concatenate([high, middle], axis=0), basis[1])
    third = narrow_dot(high, basis[2])
    small = first[2 * count :] + second[count:] + third
    return first[:count] + ((first[count : 2 * count] + second[:count]) + small)


LINES = 64
PIECES = 4
LANES = 128
TILE = 8


def form_piece(piece, ref_held, sec_held, group, hold):
    blocks = ref_held.shape[2] // LINES
    looks = LINES // LOOK_AZ
    tall = 4 * looks * blocks
    total = jnp.zeros((2 * tall, LANES), jnp.float32)
    for start in range(0, ref_held.shape[3], CHUNK):
        highs, lows = [], []
        for block in range(blocks):
            parts = []
            for begin in range(start, start + CHUNK, LANES):
                span = pl.ds(begin, LANES)
                lines = pl.ds(block * LINES, LINES)
                slot = begin // LANES * blocks + block
                mr = ref_held[piece, 0, lines, span].astype(jnp.float32)
                mi = ref_held[piece, 1, lines, span].astype(jnp.float32)
                sr = sec_held[piece, 0, lines, span].astype(jnp.float32)
                si = sec_held[piece, 1, lines, span].astype(jnp.float32)
                hold[slot, 0:LINES] = mr * sr + mi * si
                hold[slot, LINES : 2 * LINES] = mi * sr - mr * si
                hold[slot, 2 * LINES : 3 * LINES] = mr * mr + mi * mi
                hold[slot, 3 * LINES :] = sr * sr + si * si
                part = hold[slot, pl.ds(0, 4 * looks, stride=LOOK_AZ), :]
                for line in range(1, LOOK_AZ):
                    part = part + hold[slot, pl.ds(line, 4 * looks, stride=LOOK_AZ), :]
                parts.append(part)
            sums = jnp.concatenate(parts, axis=1)
            high = sums.astype(jnp.bfloat16)
            highs.append(high)
            lows.append((sums - high.astype(jnp.float32)).astype(jnp.bfloat16))
        total = total + narrow_dot(
            jnp.concatenate(highs + lows, axis=0), group[pl.ds(start, CHUNK), :]
        )
    joined = total[:tall] + total[tall:]
    planes = [
        jnp.concatenate(
            [
                joined[(4 * block + plane) * looks : (4 * block + plane + 1) * looks]
                for block in range(blocks)
            ],
            axis=0,
        )
        for plane in range(4)
    ]
    return jnp.concatenate(
        [
            planes[0] + pltpu.roll(planes[1], LANES // 2, 1),
            planes[2] + pltpu.roll(planes[3], LANES // 2, 1),
        ],
        axis=1,
    )


def unwrap_kernel(
    peers,
    capacity,
    damping,
    ref_ref,
    sec_ref,
    group_ref,
    target_ref,
    seam_ref,
    mask_ref,
    forward_ref,
    inverse_ref,
    local_ref,
    table_ref,
    couple_ref,
    out_ref,
    ref_held,
    sec_held,
    group,
    target,
    seam,
    mask,
    forward,
    inverse,
    local,
    table,
    couple,
    hold,
    place_send,
    place_recv,
    slot_send,
    slot_recv,
    grid_out,
    next_recv,
    prev_recv,
    skip_recv,
    weight,
    gammas,
    note_send,
    note_recv,
    load_sems,
    table_sems,
    place_sems,
    slot_send_sem,
    slot_sems,
    seam_send_sems,
    seam_sems,
    edge_sems,
    gamma_send_sem,
    gamma_sems,
    note_sems,
):
    me = lax.axis_index("az")
    core = lax.axis_index("rg")
    other = 1 - core
    last = peers - 1
    rows, cols = mask.shape
    length = forward.shape[1]
    slots = peers * capacity
    ends = rows + 2 * TILE
    piece_width = ref_held.shape[3]

    def at(az, rg):
        return (lax.axis_index("pass"), az, rg)

    def ahead(offset):
        return lax.rem(me + offset, peers)

    def behind(offset):
        return lax.rem(me + peers - offset, peers)

    def facing(offset):
        peer = me
        bit = 1
        while bit < peers:
            if offset & bit:
                peer = peer + bit - 2 * bit * (me // bit % 2)
            bit *= 2
        return peer

    def send(source, place, device, send_sem, recv_sem):
        pltpu.make_async_remote_copy(
            src_ref=source,
            dst_ref=place,
            send_sem=send_sem,
            recv_sem=recv_sem,
            device_id=device,
            device_id_type=pl.DeviceIdType.MESH,
        ).start()

    def settle(ref, sem):
        pltpu.make_async_copy(ref, ref, sem).wait()

    index_loads = [
        pltpu.make_async_copy(source, held, table_sems.at[number])
        for number, (source, held) in enumerate(
            ((target_ref, target), (seam_ref, seam), (mask_ref, mask), (group_ref, group))
        )
    ]
    for load in index_loads:
        load.start()
    loads = []
    for piece in range(PIECES):
        for which, (source, held) in enumerate(((ref_ref, ref_held), (sec_ref, sec_held))):
            loads.append(
                pltpu.make_async_copy(
                    source.at[:, :, pl.ds(piece * piece_width, piece_width)],
                    held.at[piece],
                    load_sems.at[2 * piece + which],
                )
            )
            loads[-1].start()
    table_loads = [
        pltpu.make_async_copy(source, held, table_sems.at[4 + number])
        for number, (source, held) in enumerate(
            (
                (forward_ref, forward),
                (inverse_ref, inverse),
                (local_ref, local),
                (table_ref, table),
                (couple_ref.at[me], couple.at[0]),
                (couple_ref.at[behind(1)], couple.at[1]),
            )
        )
    ]
    for load in table_loads:
        load.start()

    barrier = pltpu.get_barrier_semaphore()
    for offset in range(peers):
        pl.semaphore_signal(
            barrier,
            inc=1,
            device_id=at(ahead(offset), core if offset else other),
            device_id_type=pl.DeviceIdType.MESH,
        )

    def upright(line):
        diagonal = iota((rows, rows), 0) == iota((rows, rows), 1)
        return jnp.sum(jnp.where(diagonal, line, 0), axis=1, keepdims=True)

    for load in index_loads:
        load.wait()
    target_row = target[...]
    target_col = upright(target_row)
    owner_row = target_row // rows
    owner_col = target_col // rows
    same = owner_col == owner_row
    low_index = iota((rows, rows), 0)
    high_index = iota((rows, rows), 1)
    rank_row = jnp.sum(
        jnp.where(same & (low_index < high_index), 1, 0), axis=0, keepdims=True
    )
    rank_col = jnp.sum(
        jnp.where(same & (high_index < low_index), 1, 0), axis=1, keepdims=True
    )
    choose = jnp.where(
        iota((slots, rows), 0) == owner_row * capacity + rank_row, 1.0, 0.0
    ).astype(jnp.bfloat16)
    choose = jnp.concatenate([choose] * 3, axis=1)
    place = (target_col - owner_col * rows + 1).astype(jnp.float32)
    lane = iota((rows, slots), 1)
    here = lane == me * capacity + rank_col
    seam_row = seam[...]
    seam_col = upright(jnp.where(seam_row >= 0, seam_row + 1, -1)).astype(jnp.float32)
    seam_line = jnp.sum(jnp.where(lane == iota((rows, slots), 0), seam_col, 0.0), axis=0, keepdims=True)
    for dest in range(peers):
        line = jnp.sum(
            jnp.where(here & (owner_col == dest), place, 0.0), axis=0, keepdims=True
        )
        place_send[dest] = jnp.where(iota((TILE, slots), 0) == 0, line, seam_line)
    own_lanes = pl.ds(pl.multiple_of(core * cols, cols), cols)
    weight[TILE : TILE + rows, own_lanes] = (1 + mask[...]).astype(jnp.float32) * 0.25

    @pl.when(me == 0)
    def _():
        weight[0:TILE, own_lanes] = jnp.zeros((TILE, cols), jnp.float32)
        prev_recv[...] = jnp.zeros_like(prev_recv)

    @pl.when(me == last)
    def _():
        weight[TILE + rows :, own_lanes] = jnp.zeros((TILE, cols), jnp.float32)
        next_recv[...] = jnp.zeros_like(next_recv)

    @pl.when(me >= last - 1)
    def _():
        skip_recv[...] = jnp.zeros_like(skip_recv)

    first_tile, final_tile = pl.ds(TILE, TILE), pl.ds(rows, TILE)
    above_tile, below_tile = pl.ds(0, TILE), pl.ds(TILE + rows, TILE)

    def send_slots(piece):
        loads[2 * piece].wait()
        loads[2 * piece + 1].wait()
        looks = form_piece(piece, ref_held, sec_held, group, hold)
        slot_send[piece] = pick_dot(choose, looks).reshape(peers, capacity, looks.shape[1])
        if piece == 0:
            pl.semaphore_wait(barrier, peers)
            for offset in range(peers - 1, 0, -1):
                send(
                    place_send.at[facing(offset)],
                    place_recv.at[me],
                    at(facing(offset), core),
                    place_sems.at[0],
                    place_sems.at[1],
                )
            place_recv[me] = place_send[me]
        for offset in range(peers - 1, 0, -1):
            send(
                slot_send.at[piece, facing(offset)],
                slot_recv.at[piece, me],
                at(facing(offset), core),
                slot_send_sem,
                slot_sems.at[piece],
            )
        slot_recv[piece, me] = slot_send[piece, me]

    for piece in range(PIECES):
        send_slots(piece)

    @pl.when(me > 0)
    def _():
        send(
            weight.at[first_tile, own_lanes],
            weight.at[below_tile, own_lanes],
            at(behind(1), core),
            edge_sems.at[0],
            edge_sems.at[1],
        )

    @pl.when(me < last)
    def _():
        send(
            weight.at[final_tile, own_lanes],
            weight.at[above_tile, own_lanes],
            at(ahead(1), core),
            edge_sems.at[2],
            edge_sems.at[3],
        )

    settle(place_recv.at[pl.ds(0, last)], place_sems.at[1])
    places = place_recv[0][0:1]
    for source in range(1, peers):
        places = places + place_recv[source][0:1]
    seam_wanted = upright(place_recv[behind(1)][1:2, :rows])
    own_wanted = (iota((rows, slots), 0) + 1).astype(jnp.float32)
    scatter = jnp.concatenate(
        [
            jnp.where(places == seam_wanted, 1.0, 0.0),
            jnp.where(places == own_wanted, 1.0, 0.0),
        ],
        axis=0,
    ).astype(jnp.bfloat16)
    scatter = jnp.concatenate([scatter] * 3, axis=1)

    @pl.when(me < last)
    def _():
        settle(weight.at[below_tile, own_lanes], edge_sems.at[1])

    @pl.when(me > 0)
    def _():
        settle(weight.at[above_tile, own_lanes], edge_sems.at[3])

    send(
        weight.at[:, own_lanes],
        weight.at[:, own_lanes],
        at(me, other),
        edge_sems.at[4],
        edge_sems.at[5],
    )
    head = pl.ds(0, rows + TILE)
    top = pl.ds(0, TILE)
    tail = pl.ds(2 * rows - TILE, TILE)

    def send_seams(piece):
        settle(slot_recv.at[piece, pl.ds(0, last)], slot_sems.at[piece])
        arrived = slot_recv[piece].reshape(slots, 2 * LANES)
        grid_out[piece] = pick_dot(scatter, arrived)

        @pl.when(me > 0)
        def _():
            send(
                grid_out.at[piece, head],
                next_recv.at[piece],
                at(behind(1), core),
                seam_send_sems.at[0],
                seam_sems.at[0, piece],
            )

        @pl.when(me > 1)
        def _():
            send(
                grid_out.at[piece, top],
                skip_recv.at[piece],
                at(behind(2), core),
                seam_send_sems.at[1],
                seam_sems.at[1, piece],
            )

        @pl.when(me < last)
        def _():
            send(
                grid_out.at[piece, tail],
                prev_recv.at[piece],
                at(ahead(1), core),
                seam_send_sems.at[2],
                seam_sems.at[2, piece],
            )

    def send_gamma(piece):
        @pl.when(me < last)
        def _():
            settle(next_recv.at[piece], seam_sems.at[0, piece])

        @pl.when(me < last - 1)
        def _():
            settle(skip_recv.at[piece], seam_sems.at[1, piece])

        @pl.when(me > 0)
        def _():
            settle(prev_recv.at[piece], seam_sems.at[2, piece])

        own = grid_out[piece]
        coming = next_recv[piece]
        combined = jnp.concatenate(
            [
                prev_recv[piece] + own[rows - TILE : rows],
                own[rows:] + coming[:rows],
                coming[rows:] + skip_recv[piece],
            ],
            axis=0,
        )
        powers = combined[:, LANES:]
        magnitude = jnp.sqrt(powers * pltpu.roll(powers, LANES // 2, 1)) + EPSILON
        gammas[core, piece] = combined[:, :LANES] / magnitude
        send(
            gammas.at[core, piece],
            gammas.at[core, piece],
            at(me, other),
            gamma_send_sem,
            gamma_sems.at[piece],
        )

    for piece in range(PIECES):
        send_seams(piece)
        if piece:
            send_gamma(piece - 1)
    send_gamma(PIECES - 1)
    for load in table_loads:
        load.wait()
    settle(weight.at[:, own_lanes], edge_sems.at[5])

    column = iota((rows, length), 1)

    def beside(values):
        middle = values[TILE : TILE + rows]
        return (
            values[TILE - 1 : TILE - 1 + rows],
            values[TILE + 1 : TILE + 1 + rows],
            pltpu.roll(middle, 1, 1),
            pltpu.roll(middle, length - 1, 1),
        )

    weights = weight[...]
    inside = weights[TILE : TILE + rows]
    edges = [inside * item for item in beside(weights)]
    edges[2] = jnp.where(column > 0, edges[2], 0.0)
    edges[3] = jnp.where(column < length - 1, edges[3], 0.0)
    for piece in range(PIECES):
        settle(gammas.at[core, piece], gamma_sems.at[piece])
    reals, imags = [], []
    left_half = iota((ends, LANES), 1) < LANES // 2
    for side in range(2):
        for piece in range(0, PIECES, 2):
            first, second = gammas[side, piece], gammas[side, piece + 1]
            reals.append(jnp.where(left_half, first, pltpu.roll(second, LANES // 2, 1)))
            imags.append(jnp.where(left_half, pltpu.roll(first, LANES // 2, 1), second))
    real, imag = jnp.concatenate(reals, axis=1), jnp.concatenate(imags, axis=1)
    right_side = jnp.zeros((rows, length), jnp.float32)
    for edge, real_item, imag_item in zip(edges, beside(real), beside(imag)):
        right_side = right_side + edge * (
            imag[TILE : TILE + rows] * real_item - real[TILE : TILE + rows] * imag_item
        )

    def operator(values):
        middle = values[TILE : TILE + rows]
        result = damping * middle
        for edge, item in zip(edges, beside(values)):
            result = result + edge * (middle - item)
        return result

    def fold(values):
        total = None
        for row in range(0, rows, TILE):
            for begin in range(0, length, LANES):
                part = values[row : row + TILE, begin : begin + LANES]
                total = part if total is None else total + part
        return total

    def share(turn, tiles):
        for index, tile in enumerate(tiles):
            note_send[turn, index * TILE : (index + 1) * TILE] = tile
        used = pl.ds(0, len(tiles) * TILE)
        for offset in range(peers - 1, 0, -1):
            send(
                note_send.at[turn, used],
                note_recv.at[turn, me, used],
                at(facing(offset), core),
                note_sems.at[turn, 0],
                note_sems.at[turn, 1],
            )
        note_recv[turn, me, used] = note_send[turn, used]
        return used

    def collect(turn, used):
        settle(note_recv.at[turn, pl.ds(0, last), used], note_sems.at[turn, 1])

    def totals(turn, first, count):
        results = []
        for index in range(first, first + count):
            total = note_recv[turn, 0, index * TILE : (index + 1) * TILE]
            for source in range(1, peers):
                total = total + note_recv[turn, source, index * TILE : (index + 1) * TILE]
            results.append(jnp.sum(total, keepdims=True))
        return results

    forward_parts = [forward[part] for part in range(3)]
    inverse_parts = [inverse[part] for part in range(3)]
    quarter = length // LANES

    def as_row(tile):
        return jnp.concatenate([tile[index : index + 1] for index in range(quarter)], axis=1)

    def precondition(turn, values, products):
        spectrum = basis_dot(values, forward_parts)
        from_top, from_end, inverted = table[0], table[1], table[2]
        first = jnp.sum(spectrum * from_top, axis=0, keepdims=True)
        final = jnp.sum(spectrum * from_end, axis=0, keepdims=True)
        rims = jnp.concatenate(
            [
                line[:, begin : begin + LANES]
                for line in (first, final)
                for begin in range(0, length, LANES)
            ],
            axis=0,
        )
        used = share(turn, [rims] + [fold(product) for product in products])
        alone = left_dot(local[1], left_dot(local[0], spectrum) * inverted)
        collect(turn, used)
        jumps = []
        for which in range(2):
            total = couple[which, 0] * note_recv[turn, 0, 0:TILE]
            for source in range(1, peers):
                total = total + couple[which, source] * note_recv[turn, source, 0:TILE]
            jumps.append(as_row(total[:quarter] + total[quarter:]))
        below, above = jumps
        solved = alone - from_end * below + from_top * above
        padded = jnp.concatenate(
            [
                jnp.broadcast_to(solved[0:1] + above, (TILE, length)),
                solved,
                jnp.broadcast_to(solved[rows - 1 :] - below, (TILE, length)),
            ],
            axis=0,
        )
        return basis_dot(padded, inverse_parts)

    z0 = precondition(0, right_side, [])
    z0_mid = z0[TILE : TILE + rows]
    w0 = operator(z0)
    y0 = precondition(1, w0, [right_side * z0_mid, z0_mid * w0])
    rho0, energy0 = totals(1, 1, 2)
    alpha0 = rho0 / energy0
    r1 = right_side - alpha0 * w0
    z1 = z0 - alpha0 * y0
    z1_mid = z1[TILE : TILE + rows]
    q1 = operator(z1)
    collect(2, share(2, [fold(r1 * z1_mid), fold(z1_mid * q1), fold(z0_mid * q1)]))
    rho1, energy1, cross = totals(2, 0, 3)
    beta = rho1 / rho0
    alpha1 = rho1 / (energy1 + 2.0 * beta * cross + beta * beta * energy0)
    answer = alpha0 * z0_mid + alpha1 * (z1_mid + beta * z0_mid)
    left = r1 - alpha1 * (q1 + beta * w0)
    out_ref[0] = jnp.where(core == 0, answer[:, :cols], answer[:, cols:])
    out_ref[1] = jnp.where(core == 0, left[:, :cols], left[:, cols:])

    settle(place_send.at[pl.ds(0, last)], place_sems.at[0])
    settle(slot_send.at[:, pl.ds(0, last)], slot_send_sem)
    settle(weight.at[:, own_lanes], edge_sems.at[4])
    settle(gammas.at[core], gamma_send_sem)
    settle(note_recv.at[0, pl.ds(0, last), top], note_sems.at[0, 0])
    settle(note_recv.at[1, pl.ds(0, last)], note_sems.at[1, 0])
    settle(note_recv.at[2, pl.ds(0, last)], note_sems.at[2, 0])

    @pl.when(me > 0)
    def _():
        settle(weight.at[first_tile, own_lanes], edge_sems.at[0])
        settle(grid_out.at[:, head], seam_send_sems.at[0])

    @pl.when(me > 1)
    def _():
        settle(grid_out.at[:, top], seam_send_sems.at[1])

    @pl.when(me < last)
    def _():
        settle(weight.at[final_tile, own_lanes], edge_sems.at[2])
        settle(grid_out.at[:, tail], seam_send_sems.at[2])


def fits_kernel(peers, cores, rows, cols):
    length = rows * peers
    capacity = max(2, 2 * rows // peers)
    return (
        cores == 2
        and rows == 64
        and length == cols * cores
        and length == 4 * LANES
        and peers * capacity == LANES
        and peers == TILE
    )


def dct_matrix(length):
    freq = np.arange(length)
    angle = (2 * freq[None, :] + 1) * freq[:, None] % (4 * length)
    scale = np.sqrt(np.where(freq == 0, 1.0, 2.0) / length)
    return scale[:, None] * np.cos(angle * (math.pi / (2.0 * length)))


def exact_eigenvalues(length):
    return 4.0 * np.sin(np.arange(length) * (math.pi / (2.0 * length))) ** 2


def bf16_parts(matrix):
    parts, rest = [], matrix
    for _ in range(3):
        parts.append(rest.astype(jnp.bfloat16))
        rest = rest - parts[-1].astype(np.float64)
    return parts


def left_parts(matrix):
    first, second, third = bf16_parts(matrix)
    return np.concatenate([first, second, third, first, second, first], axis=1)


def solve_tables(peers, rows, length, damping):
    small = dct_matrix(rows)
    shift = exact_eigenvalues(length) + damping
    inverted = 1.0 / (exact_eigenvalues(rows)[:, None] + shift[None, :])
    from_top = small.T @ (small[:, 0:1] * inverted)
    near, far = from_top[0], from_top[-1]
    count = peers - 1
    system = np.zeros((length, count, count))
    for index in range(count):
        system[:, index, index] = 1.0 + 2.0 * near
        if index:
            system[:, index, index - 1] = -far
            system[:, index - 1, index] = -far
    solved = np.linalg.inv(system)
    couple = np.zeros((peers, peers, 2, length))
    for jump in range(count):
        for index in range(count):
            couple[jump, index, 1] += solved[:, jump, index]
            couple[jump, index + 1, 0] -= solved[:, jump, index]
    tables = np.stack([from_top, from_top[::-1], inverted]).astype(np.float32)
    couple = couple.reshape(peers, peers, 2 * length // LANES, LANES).astype(np.float32)
    return np.stack([left_parts(small), left_parts(small.T)]), tables, couple


def unwrap_in_kernel(reference_slc, secondary_slc, line_target, seam_partner, mask_level, peers):
    rows, cols = mask_level.shape
    length = rows * peers
    capacity = max(2, 2 * rows // peers)
    slots = peers * capacity
    damping = 0.25 / (rows * rows)
    basis = dct_matrix(length)
    inverse = np.stack(bf16_parts(basis))
    forward = np.stack(bf16_parts(basis.T))
    local, tables, couple = solve_tables(peers, rows, length, damping)
    width = reference_slc.shape[2] // PIECES
    lines = reference_slc.shape[1]
    group = (np.arange(width)[:, None] // LOOK_RG == np.arange(LANES)[None, :]).astype(jnp.bfloat16)
    hbm = pl.BlockSpec(memory_space=pl.ANY)
    vmem = pl.BlockSpec(memory_space=pltpu.VMEM)
    dma = pltpu.SemaphoreType.DMA

    def scratch(*dims):
        return pltpu.VMEM(dims, jnp.float32)

    def like(array):
        return pltpu.VMEM(array.shape, array.dtype)

    target, seam = line_target.reshape(1, rows), seam_partner.reshape(1, rows)
    both = pl.pallas_call(
        functools.partial(unwrap_kernel, peers, capacity, damping),
        out_shape=jax.ShapeDtypeStruct((2, rows, cols), jnp.float32),
        in_specs=[hbm] * 11,
        out_specs=vmem,
        scratch_shapes=[
            pltpu.VMEM((PIECES, 2, lines, width), jnp.bfloat16),
            pltpu.VMEM((PIECES, 2, lines, width), jnp.bfloat16),
            like(group),
            like(target),
            like(seam),
            like(mask_level),
            like(forward),
            like(inverse),
            like(local),
            like(tables),
            scratch(2, peers, TILE, LANES),
            scratch(width // LANES * (lines // LINES), 4 * LINES, LANES),
            scratch(peers, TILE, slots),
            scratch(peers, TILE, slots),
            scratch(PIECES, peers, capacity, 2 * LANES),
            scratch(PIECES, peers, capacity, 2 * LANES),
            scratch(PIECES, 2 * rows, 2 * LANES),
            scratch(PIECES, rows + TILE, 2 * LANES),
            scratch(PIECES, TILE, 2 * LANES),
            scratch(PIECES, TILE, 2 * LANES),
            scratch(rows + 2 * TILE, length),
            scratch(2, PIECES, rows + 2 * TILE, LANES),
            scratch(3, 3 * TILE, LANES),
            scratch(3, peers, 3 * TILE, LANES),
            dma((2 * PIECES,)),
            dma((10,)),
            dma((2,)),
            dma,
            dma((PIECES,)),
            dma((3,)),
            dma((3, PIECES)),
            dma((6,)),
            dma,
            dma((PIECES,)),
            dma((3, 2)),
        ],
        compiler_params=pltpu.CompilerParams(
            collective_id=0, has_side_effects=True, vmem_limit_bytes=63 * 2**20
        ),
        name="unwrap",
    )(
        reference_slc,
        secondary_slc,
        group,
        target,
        seam,
        mask_level,
        forward,
        inverse,
        local,
        tables,
        couple,
    )
    shape = jax.ShapeDtypeStruct((rows, cols), jnp.float32)
    return pl.pallas_call(
        part_kernel,
        out_shape=(shape, shape),
        in_specs=[vmem],
        out_specs=(vmem, vmem),
        name="part",
    )(both)


def part_kernel(both_ref, first_ref, second_ref):
    first_ref[...] = both_ref[0]
    second_ref[...] = both_ref[1]


def pick_rows(wanted, stack):
    choose = (wanted[:, None] == jnp.arange(stack.shape[1], dtype=jnp.int32)).astype(jnp.float32)
    return jnp.einsum("sr,prc->psc", choose, stack, precision=FULL_PRECISION)


def single_product(left, right):
    return lax.psum(jnp.sum(left * right), ("az", "rg"))


def on_device(reference_slc, secondary_slc, line_target, seam_partner, mask_level):
    dev_count = lax.axis_size("az")
    rg_count = lax.axis_size("rg")
    az_place = lax.axis_index("az")
    rg_place = lax.axis_index("rg")
    row_count = line_target.shape[0]
    col_count = mask_level.shape[1]
    if fits_kernel(dev_count, rg_count, row_count, col_count):
        return unwrap_in_kernel(
            reference_slc, secondary_slc, line_target, seam_partner, mask_level, dev_count
        )
    local_sums = form_looks(reference_slc, secondary_slc, col_count)
    capacity = max(2, 2 * row_count // dev_count)
    owners = line_target // row_count
    local_index = jnp.arange(row_count, dtype=jnp.int32)
    earlier = (owners[:, None] == owners[None, :]) & (local_index[None, :] < local_index[:, None])
    slot_rank = jnp.sum(earlier.astype(jnp.int32), axis=1)
    slot_index = owners * capacity + slot_rank
    buffer_length = dev_count * capacity
    source_row = jnp.full((buffer_length,), row_count, jnp.int32).at[slot_index].set(local_index)
    positions = (
        jnp.full((1, buffer_length), row_count, jnp.int32)
        .at[0, slot_index]
        .set(line_target % row_count)
    )
    sent_sums = pick_rows(source_row, local_sums)
    got_sums, got_positions = (
        lax.all_to_all(sent_sums, "az", split_axis=1, concat_axis=1, tiled=True),
        lax.all_to_all(positions, "az", split_axis=1, concat_axis=1, tiled=True),
    )
    gridded = jnp.zeros_like(local_sums).at[:, got_positions[0]].set(got_sums, mode="drop")
    next_block = from_behind(gridded, "az", -1)
    combined = gridded + pick_rows(seam_partner, next_block)
    magnitude = jnp.sqrt(combined[2] * combined[3]) + EPSILON
    weight = (1 + mask_level).astype(jnp.float32) * 0.25
    fields = jnp.stack([combined[0] / magnitude, combined[1] / magnitude, weight])
    padded = with_halo(fields, (("az", 1), ("rg", 2)), 1)
    beside_all = neighbours(padded)
    edge_weights = [weight * item[2] for item in beside_all]
    right_side = jnp.zeros((row_count, col_count), jnp.float32)
    for edge, item in zip(edge_weights, beside_all):
        right_side = right_side + edge * (fields[1] * item[0] - fields[0] * item[1])
    damping = 0.25 / (row_count * row_count)
    grid_rows = row_count * dev_count
    grid_cols = col_count * rg_count
    my_cols = rg_place * col_count + jnp.arange(col_count, dtype=jnp.int32)
    column_width = col_count // dev_count
    all_rows = jnp.arange(grid_rows, dtype=jnp.int32)
    full_basis = dct_table(all_rows, all_rows, grid_rows)
    pencil_cols = (
        rg_place * col_count + az_place * column_width + jnp.arange(column_width, dtype=jnp.int32)
    )
    pencil_divisor = (
        eigenvalues(pencil_cols, grid_cols)[:, None]
        + eigenvalues(all_rows, grid_rows)[None, :]
        + damping
    )

    def precondition(values):
        basis_block = dct_table(
            jnp.arange(col_count * lax.axis_size("rg"), dtype=jnp.int32), my_cols, grid_cols
        )
        range_spectrum = lax.psum_scatter(
            contract(basis_block, values, 1, 1), "rg", scatter_dimension=0, tiled=True
        )
        pencil = lax.all_to_all(range_spectrum, "az", split_axis=0, concat_axis=1, tiled=True)
        filtered = contract(pencil, full_basis, 1, 1) / pencil_divisor
        restored = contract(filtered, full_basis, 1, 0)
        back_columns = lax.all_to_all(restored, "az", split_axis=1, concat_axis=0, tiled=True)
        basis_block = dct_table(
            my_cols, jnp.arange(col_count * lax.axis_size("rg"), dtype=jnp.int32), grid_cols
        )
        return lax.psum_scatter(
            contract(basis_block, back_columns, 0, 0), "rg", scatter_dimension=0, tiled=True
        ).T

    solution = jnp.zeros((row_count, col_count), jnp.float32)
    residual = right_side
    precond = precondition(residual)
    direction = precond
    inner_now = single_product(residual, precond)
    for turn_index in range(ITERS):
        rim = with_halo(direction, (("az", 0), ("rg", 1)), 1)
        result_sum = damping * direction
        for apply_edge, apply_item in zip(edge_weights, neighbours(rim)):
            result_sum = result_sum + apply_edge * (direction - apply_item)
        step_size = inner_now / lax.psum(jnp.sum(direction * result_sum), ("az", "rg"))
        solution = solution + step_size * direction
        residual = residual - step_size * result_sum
        if turn_index + 1 < ITERS:
            precond = precondition(residual)
            inner_next = single_product(residual, precond)
            direction = precond + inner_next / inner_now * direction
            inner_now = inner_next
    return (solution, residual)


def solution(mesh):
    in_specs = (
        P(None, ("pass", "az"), "rg"),
        P(None, ("pass", "az"), "rg"),
        P(("pass", "az")),
        P(("pass", "az")),
        P(("pass", "az"), "rg"),
    )
    out_specs = (P(("pass", "az"), "rg"), P(("pass", "az"), "rg"))
    return jax.shard_map(
        on_device, mesh=mesh, in_specs=in_specs, out_specs=out_specs, check_vma=False
    )
```

```python
import functools
import math

import jax
import jax.numpy as jnp
import numpy as np
from jax import lax
from jax.experimental import pallas as pl
from jax.experimental.pallas import tpu as pltpu
from jax.sharding import PartitionSpec as P

LOOK_AZ = 4
LOOK_RG = 20
ITERS = 2


FULL_PRECISION = lax.Precision.HIGHEST
EPSILON = 1e-06


def from_behind(value, axis, steps):
    count = lax.axis_size(axis)
    first, last = (max(0, -steps), min(count, count - steps))
    return lax.ppermute(value, axis, [(source, source + steps) for source in range(first, last)])


def with_halo(shard, sides, width):
    for axis, dim in sides:
        peers, length = (lax.axis_size(axis), shard.shape[dim])
        up = [(i, (i + 1) % peers) for i in range(peers - 1)]
        down = [(j, i) for i, j in up]
        last = lax.slice_in_dim(shard, length - width, length, axis=dim)
        first = lax.slice_in_dim(shard, 0, width, axis=dim)
        before = lax.ppermute(last, axis, up)
        after = lax.ppermute(first, axis, down)
        shard = jnp.concatenate([before, shard, after], axis=dim)
    return shard


def dct_table(freq_index, place_index, length):
    product = (2 * place_index[None, :] + 1) * freq_index[:, None] % (4 * length)
    norm_factor = jnp.where(
        freq_index == 0, math.sqrt(1.0 / length), math.sqrt(2.0 / length)
    ).astype(jnp.float32)
    return norm_factor[:, None] * jnp.cos(product.astype(jnp.float32) * (math.pi / (2.0 * length)))


def eigenvalues(freq_index, length):
    return 4.0 * jnp.sin(freq_index.astype(jnp.float32) * (math.pi / (2.0 * length))) ** 2


def neighbours(padded):
    return (
        padded[..., :-2, 1:-1],
        padded[..., 2:, 1:-1],
        padded[..., 1:-1, :-2],
        padded[..., 1:-1, 2:],
    )


def contract(left, right, left_dim, right_dim):
    return lax.dot_general(
        left,
        right,
        (((left_dim,), (right_dim,)), ((), ())),
        precision=FULL_PRECISION,
        preferred_element_type=jnp.float32,
    )


CHUNK = 256


def look_kernel(lines, half, ref_ref, sec_ref, group_ref, line_ref, out_ref):
    step_rows = lines // LOOK_AZ
    width = half // LOOK_RG
    for side in range(out_ref.shape[2] // width):
        total = jnp.zeros((8 * lines, width), jnp.float32)
        for start in range(0, half, CHUNK):
            span = pl.ds(side * half + start, CHUNK)
            mr = ref_ref[0, :, span].astype(jnp.float32)
            mi = ref_ref[1, :, span].astype(jnp.float32)
            sr = sec_ref[0, :, span].astype(jnp.float32)
            si = sec_ref[1, :, span].astype(jnp.float32)
            planes = jnp.concatenate(
                [mr * sr + mi * si, mi * sr - mr * si, mr * mr + mi * mi, sr * sr + si * si], axis=0
            )
            high = planes.astype(jnp.bfloat16)
            low = (planes - high.astype(jnp.float32)).astype(jnp.bfloat16)
            total = total + jnp.dot(
                jnp.concatenate([high, low], axis=0),
                group_ref[pl.ds(start, CHUNK), :],
                preferred_element_type=jnp.float32,
            )
        joined = total[: 4 * lines] + total[4 * lines :]
        sums = jnp.dot(
            line_ref[...], joined, precision=FULL_PRECISION, preferred_element_type=jnp.float32
        )
        for plane in range(4):
            out_ref[plane, :, side * width : (side + 1) * width] = sums[
                plane * step_rows : (plane + 1) * step_rows
            ]


def form_looks(ref_lines, sec_lines, col_count):
    line_count, sample_count = ref_lines.shape[1:]
    lines = 32
    half = 128 * LOOK_RG
    group = (np.arange(half)[:, None] // LOOK_RG == np.arange(128)[None, :]).astype(jnp.bfloat16)
    line_of = (np.arange(4 * lines)[None, :] // LOOK_AZ == np.arange(lines)[:, None]).astype(
        np.float32
    )
    block = pl.BlockSpec((2, lines, sample_count), lambda i: (0, i, 0))
    return pl.pallas_call(
        functools.partial(look_kernel, lines, half),
        grid=(line_count // lines,),
        in_specs=[
            block,
            block,
            pl.BlockSpec(group.shape, lambda i: (0, 0)),
            pl.BlockSpec(line_of.shape, lambda i: (0, 0)),
        ],
        out_specs=pl.BlockSpec((4, lines // LOOK_AZ, col_count), lambda i: (0, i, 0)),
        out_shape=jax.ShapeDtypeStruct((4, line_count // LOOK_AZ, col_count), jnp.float32),
        name="form_looks",
    )(ref_lines, sec_lines, group, line_of)


def iota(shape, dim):
    return lax.broadcasted_iota(jnp.int32, shape, dim)


def split(values):
    high = values.astype(jnp.bfloat16)
    rest = values - high.astype(jnp.float32)
    middle = rest.astype(jnp.bfloat16)
    return high, middle, (rest - middle.astype(jnp.float32)).astype(jnp.bfloat16)


def narrow_dot(left, right):
    return jnp.dot(left, right, preferred_element_type=jnp.float32)


def pick_dot(choose_thrice, values):
    return narrow_dot(choose_thrice, jnp.concatenate(split(values), axis=0))


def left_dot(parts, values):
    high, middle, low = split(values)
    return narrow_dot(parts, jnp.concatenate([low, middle, high, middle, high, high], axis=0))


def basis_dot(values, basis):
    count = values.shape[0]
    high, middle, low = split(values)
    first = narrow_dot(jnp.concatenate([high, middle, low], axis=0), basis[0])
    second = narrow_dot(jnp.concatenate([high, middle], axis=0), basis[1])
    third = narrow_dot(high, basis[2])
    small = first[2 * count :] + second[count:] + third
    return first[:count] + ((first[count : 2 * count] + second[:count]) + small)


LINES = 64
PIECES = 8
PART = 32
LAG = 6
LANES = 128
TILE = 8


def form_piece(piece, held, group, hold):
    lines_held, width = held.shape[3:]
    blocks = lines_held // LINES
    looks = LINES // LOOK_AZ
    tall = 4 * looks * blocks
    total = jnp.zeros((2 * tall, LANES), jnp.float32)
    for start in range(0, width, CHUNK):
        end = min(start + CHUNK, width)
        highs, lows = [], []
        for block in range(blocks):
            parts = []
            for begin in range(start, end, LANES):
                span = pl.ds(begin, LANES)
                lines = pl.ds(block * LINES, LINES)
                slot = begin // LANES * blocks + block
                mr = held[piece, 0, 0, lines, span].astype(jnp.float32)
                mi = held[piece, 0, 1, lines, span].astype(jnp.float32)
                sr = held[piece, 1, 0, lines, span].astype(jnp.float32)
                si = held[piece, 1, 1, lines, span].astype(jnp.float32)
                hold[slot, 0:LINES] = mr * sr + mi * si
                hold[slot, LINES : 2 * LINES] = mi * sr - mr * si
                hold[slot, 2 * LINES : 3 * LINES] = mr * mr + mi * mi
                hold[slot, 3 * LINES :] = sr * sr + si * si
                part = hold[slot, pl.ds(0, 4 * looks, stride=LOOK_AZ), :]
                for line in range(1, LOOK_AZ):
                    part = part + hold[slot, pl.ds(line, 4 * looks, stride=LOOK_AZ), :]
                parts.append(part)
            sums = jnp.concatenate(parts, axis=1)
            high = sums.astype(jnp.bfloat16)
            highs.append(high)
            lows.append((sums - high.astype(jnp.float32)).astype(jnp.bfloat16))
        total = total + narrow_dot(
            jnp.concatenate(highs + lows, axis=0), group[start:end, :]
        )
    joined = total[:tall] + total[tall:]
    tile = None
    for plane in range(4):
        part = jnp.concatenate(
            [
                joined[(4 * block + plane) * looks : (4 * block + plane + 1) * looks]
                for block in range(blocks)
            ],
            axis=0,
        )
        tile = part if plane == 0 else tile + pltpu.roll(part, plane * PART, 1)
    return tile


def unwrap_kernel(
    peers,
    capacity,
    damping,
    ref_ref,
    sec_ref,
    group_ref,
    target_ref,
    seam_ref,
    mask_ref,
    forward_ref,
    inverse_ref,
    local_ref,
    table_ref,
    couple_ref,
    out_ref,
    held,
    group,
    target,
    seam,
    mask,
    forward,
    inverse,
    local,
    table,
    couple,
    hold,
    place_send,
    place_recv,
    slot_send,
    slot_recv,
    grid_out,
    seam_recv,
    weight,
    fields,
    note_send,
    note_recv,
    load_sems,
    table_sems,
    place_sems,
    slot_send_sem,
    slot_sems,
    seam_send_sems,
    seam_sems,
    edge_sems,
    gamma_send_sem,
    gamma_sems,
    note_sems,
):
    me = lax.axis_index("az")
    core = lax.axis_index("rg")
    other = 1 - core
    last = peers - 1
    rows, cols = mask.shape
    length = forward.shape[1]
    slots = peers * capacity
    ends = rows + 2 * TILE
    after, beyond, before = pl.ds(0, rows + TILE), pl.ds(rows + TILE, TILE), pl.ds(ends, TILE)
    piece_width = held.shape[4]

    def at(az, rg):
        return (lax.axis_index("pass"), az, rg)

    def ahead(offset):
        return lax.rem(me + offset, peers)

    def behind(offset):
        return lax.rem(me + peers - offset, peers)

    def facing(offset):
        peer = me
        bit = 1
        while bit < peers:
            if offset & bit:
                peer = peer + bit - 2 * bit * (me // bit % 2)
            bit *= 2
        return peer

    def send(source, place, device, send_sem, recv_sem):
        pltpu.make_async_remote_copy(
            src_ref=source,
            dst_ref=place,
            send_sem=send_sem,
            recv_sem=recv_sem,
            device_id=device,
            device_id_type=pl.DeviceIdType.MESH,
        ).start()

    def settle(ref, sem):
        pltpu.make_async_copy(ref, ref, sem).wait()

    barrier = pltpu.get_barrier_semaphore()
    for offset in range(peers - 1, -1, -1):
        pl.semaphore_signal(
            barrier,
            inc=1,
            device_id=at(facing(offset), core if offset else other),
            device_id_type=pl.DeviceIdType.MESH,
        )

    index_loads = [
        pltpu.make_async_copy(source, held, table_sems.at[number])
        for number, (source, held) in enumerate(
            ((target_ref, target), (seam_ref, seam), (mask_ref, mask), (group_ref, group))
        )
    ]
    for load in index_loads:
        load.start()
    for piece in range(PIECES):
        for which, source in enumerate((ref_ref, sec_ref)):
            pltpu.make_async_copy(
                source.at[:, :, pl.ds(piece * piece_width, piece_width)],
                held.at[piece, which],
                load_sems.at[piece],
            ).start()
    table_loads = [
        pltpu.make_async_copy(source, held, table_sems.at[4 + number])
        for number, (source, held) in enumerate(
            (
                (forward_ref, forward),
                (inverse_ref, inverse),
                (local_ref, local),
                (table_ref, table),
                (couple_ref.at[me], couple.at[0]),
                (couple_ref.at[behind(1)], couple.at[1]),
            )
        )
    ]
    for load in table_loads:
        load.start()

    def upright(line):
        diagonal = iota((rows, rows), 0) == iota((rows, rows), 1)
        return jnp.sum(jnp.where(diagonal, line, 0), axis=1, keepdims=True)

    for load in index_loads:
        load.wait()
    target_row = target[...]
    target_col = upright(target_row)
    owner_row = target_row // rows
    owner_col = target_col // rows
    same = owner_col == owner_row
    low_index = iota((rows, rows), 0)
    high_index = iota((rows, rows), 1)
    rank_row = jnp.sum(
        jnp.where(same & (low_index < high_index), 1, 0), axis=0, keepdims=True
    )
    rank_col = jnp.sum(
        jnp.where(same & (high_index < low_index), 1, 0), axis=1, keepdims=True
    )
    choose = jnp.where(
        iota((slots, rows), 0) == owner_row * capacity + rank_row, 1.0, 0.0
    ).astype(jnp.bfloat16)
    choose = jnp.concatenate([choose] * 3, axis=1)
    own_lanes = pl.ds(pl.multiple_of(core * cols, cols), cols)
    weight[TILE : TILE + rows, own_lanes] = (1 + mask[...]).astype(jnp.float32) * 0.25

    @pl.when(me == 0)
    def _():
        weight[0:TILE, own_lanes] = jnp.zeros((TILE, cols), jnp.float32)
        seam_recv[:, before] = jnp.zeros((PIECES, TILE, LANES), jnp.float32)

    @pl.when(me == last)
    def _():
        weight[TILE + rows :, own_lanes] = jnp.zeros((TILE, cols), jnp.float32)
        seam_recv[:, after] = jnp.zeros((PIECES, rows + TILE, LANES), jnp.float32)

    @pl.when(me >= last - 1)
    def _():
        seam_recv[:, beyond] = jnp.zeros((PIECES, TILE, LANES), jnp.float32)

    def fill_places():
        place = (target_col - owner_col * rows + 1).astype(jnp.float32)
        lane = iota((rows, slots), 1)
        here = lane == me * capacity + rank_col
        seam_row = seam[...]
        seam_col = upright(jnp.where(seam_row >= 0, seam_row + 1, -1)).astype(jnp.float32)
        seam_line = jnp.sum(jnp.where(lane == iota((rows, slots), 0), seam_col, 0.0), axis=0, keepdims=True)
        for dest in range(peers):
            line = jnp.sum(
                jnp.where(here & (owner_col == dest), place, 0.0), axis=0, keepdims=True
            )
            place_send[dest] = jnp.where(iota((TILE, slots), 0) == 0, line, seam_line)

    first_tile, final_tile = pl.ds(TILE, TILE), pl.ds(rows, TILE)
    above_tile, below_tile = pl.ds(0, TILE), pl.ds(TILE + rows, TILE)

    def send_slots(piece):
        settle(held.at[piece], load_sems.at[piece])
        looks = form_piece(piece, held, group, hold)
        slot_send[piece] = pick_dot(choose, looks).reshape(peers, capacity, LANES)
        if piece == 0:
            pl.semaphore_wait(barrier, peers)
        for offset in range(peers - 1, 0, -1):
            send(
                slot_send.at[piece, facing(offset)],
                slot_recv.at[piece, me],
                at(facing(offset), core),
                slot_send_sem,
                slot_sems.at[piece],
            )
        slot_recv[piece, me] = slot_send[piece, me]
        if piece == 0:
            fill_places()
            for offset in range(peers - 1, 0, -1):
                send(
                    place_send.at[facing(offset)],
                    place_recv.at[me],
                    at(facing(offset), core),
                    place_sems.at[0],
                    place_sems.at[1],
                )
            place_recv[me] = place_send[me]

    for piece in range(PIECES):
        send_slots(piece)

    @pl.when(me > 0)
    def _():
        send(
            weight.at[first_tile, own_lanes],
            weight.at[below_tile, own_lanes],
            at(behind(1), core),
            edge_sems.at[0],
            edge_sems.at[1],
        )

    @pl.when(me < last)
    def _():
        send(
            weight.at[final_tile, own_lanes],
            weight.at[above_tile, own_lanes],
            at(ahead(1), core),
            edge_sems.at[2],
            edge_sems.at[3],
        )

    settle(place_recv.at[pl.ds(0, last)], place_sems.at[1])
    places = place_recv[0][0:1]
    for source in range(1, peers):
        places = places + place_recv[source][0:1]
    seam_wanted = upright(place_recv[behind(1)][1:2, :rows])
    own_wanted = (iota((rows, slots), 0) + 1).astype(jnp.float32)
    scatter = jnp.concatenate(
        [
            jnp.where(places == seam_wanted, 1.0, 0.0),
            jnp.where(places == own_wanted, 1.0, 0.0),
        ],
        axis=0,
    ).astype(jnp.bfloat16)
    scatter = jnp.concatenate([scatter] * 3, axis=1)

    @pl.when(me < last)
    def _():
        settle(weight.at[below_tile, own_lanes], edge_sems.at[1])

    @pl.when(me > 0)
    def _():
        settle(weight.at[above_tile, own_lanes], edge_sems.at[3])

    send(
        weight.at[:, own_lanes],
        weight.at[:, own_lanes],
        at(me, other),
        edge_sems.at[4],
        edge_sems.at[5],
    )
    head = pl.ds(0, rows + TILE)
    top = pl.ds(0, TILE)
    tail = pl.ds(2 * rows - TILE, TILE)

    def send_seams(piece):
        settle(slot_recv.at[piece, pl.ds(0, last)], slot_sems.at[piece])
        arrived = slot_recv[piece].reshape(slots, LANES)
        grid_out[piece] = pick_dot(scatter, arrived)

        @pl.when(me > 0)
        def _():
            send(
                grid_out.at[piece, head],
                seam_recv.at[piece, after],
                at(behind(1), core),
                seam_send_sems.at[0],
                seam_sems.at[piece],
            )

        @pl.when(me > 1)
        def _():
            send(
                grid_out.at[piece, top],
                seam_recv.at[piece, beyond],
                at(behind(2), core),
                seam_send_sems.at[1],
                seam_sems.at[piece],
            )

        @pl.when(me < last)
        def _():
            send(
                grid_out.at[piece, tail],
                seam_recv.at[piece, before],
                at(ahead(1), core),
                seam_send_sems.at[2],
                seam_sems.at[piece],
            )

    part_of = iota((ends, LANES), 1) // PART

    def send_gamma(piece, planes):
        @pl.when((me > 0) & (me < last - 1))
        def _():
            settle(seam_recv.at[piece], seam_sems.at[piece])

        @pl.when((me == 0) | (me == last - 1))
        def _():
            settle(seam_recv.at[piece, pl.ds(0, ends)], seam_sems.at[piece])

        @pl.when(me == last)
        def _():
            settle(seam_recv.at[piece, before], seam_sems.at[piece])

        own = grid_out[piece]
        coming = seam_recv[piece]
        combined = jnp.concatenate(
            [
                coming[ends:] + own[rows - TILE : rows],
                own[rows:] + coming[:rows],
                coming[rows : rows + TILE] + coming[rows + TILE : ends],
            ],
            axis=0,
        )
        magnitude = jnp.sqrt(combined * pltpu.roll(combined, PART, 1)) + EPSILON
        magnitude = jnp.where(
            part_of == 0, pltpu.roll(magnitude, PART, 1), pltpu.roll(magnitude, 2 * PART, 1)
        )
        gamma = combined / magnitude
        tile, spot = piece * PART // LANES, piece % (LANES // PART)
        for plane in range(2):
            moved = (spot - plane) * PART % LANES
            part = pltpu.roll(gamma, moved, 1) if moved else gamma
            planes[plane] = jnp.where(part_of == spot, part, planes[plane]) if spot else part
        if spot == LANES // PART - 1:
            place = core * (cols // LANES) + tile
            for plane in range(2):
                fields[plane, place] = planes[plane]
            send(
                fields.at[:, place],
                fields.at[:, place],
                at(me, other),
                gamma_send_sem,
                gamma_sems.at[tile],
            )

    planes = [None, None]
    for piece in range(PIECES + LAG):
        if piece < PIECES:
            send_seams(piece)
        if piece >= LAG:
            send_gamma(piece - LAG, planes)
    for load in table_loads:
        load.wait()
    settle(weight.at[:, own_lanes], edge_sems.at[5])

    column = iota((rows, length), 1)

    def beside(values):
        middle = values[TILE : TILE + rows]
        return (
            values[TILE - 1 : TILE - 1 + rows],
            values[TILE + 1 : TILE + 1 + rows],
            pltpu.roll(middle, 1, 1),
            pltpu.roll(middle, length - 1, 1),
        )

    weights = weight[...]
    inside = weights[TILE : TILE + rows]
    edges = [inside * item for item in beside(weights)]
    edges[2] = jnp.where(column > 0, edges[2], 0.0)
    edges[3] = jnp.where(column < length - 1, edges[3], 0.0)
    tiles = cols // LANES
    for tile in range(tiles):
        settle(fields.at[:, tile], gamma_sems.at[tile])
    real, imag = [
        jnp.concatenate([fields[plane, tile] for tile in range(2 * tiles)], axis=1)
        for plane in range(2)
    ]
    right_side = jnp.zeros((rows, length), jnp.float32)
    for edge, real_item, imag_item in zip(edges, beside(real), beside(imag)):
        right_side = right_side + edge * (
            imag[TILE : TILE + rows] * real_item - real[TILE : TILE + rows] * imag_item
        )

    def operator(values):
        middle = values[TILE : TILE + rows]
        result = damping * middle
        for edge, item in zip(edges, beside(values)):
            result = result + edge * (middle - item)
        return result

    def fold(values):
        total = None
        for row in range(0, rows, TILE):
            for begin in range(0, length, LANES):
                part = values[row : row + TILE, begin : begin + LANES]
                total = part if total is None else total + part
        return total

    def share(turn, tiles):
        for index, tile in enumerate(tiles):
            note_send[turn, index * TILE : (index + 1) * TILE] = tile
        used = pl.ds(0, len(tiles) * TILE)
        for offset in range(peers - 1, 0, -1):
            send(
                note_send.at[turn, used],
                note_recv.at[turn, me, used],
                at(facing(offset), core),
                note_sems.at[turn, 0],
                note_sems.at[turn, 1],
            )
        note_recv[turn, me, used] = note_send[turn, used]
        return used

    def collect(turn, used):
        settle(note_recv.at[turn, pl.ds(0, last), used], note_sems.at[turn, 1])

    def totals(turn, first, count):
        results = []
        for index in range(first, first + count):
            total = note_recv[turn, 0, index * TILE : (index + 1) * TILE]
            for source in range(1, peers):
                total = total + note_recv[turn, source, index * TILE : (index + 1) * TILE]
            results.append(jnp.sum(total, keepdims=True))
        return results

    forward_parts = [forward[part] for part in range(3)]
    inverse_parts = [inverse[part] for part in range(3)]
    quarter = length // LANES

    def as_row(tile):
        return jnp.concatenate([tile[index : index + 1] for index in range(quarter)], axis=1)

    def precondition(turn, values, products):
        spectrum = basis_dot(values, forward_parts)
        from_top, from_end, inverted = table[0], table[1], table[2]
        first = jnp.sum(spectrum * from_top, axis=0, keepdims=True)
        final = jnp.sum(spectrum * from_end, axis=0, keepdims=True)
        rims = jnp.concatenate(
            [
                line[:, begin : begin + LANES]
                for line in (first, final)
                for begin in range(0, length, LANES)
            ],
            axis=0,
        )
        used = share(turn, [rims] + [fold(product) for product in products])
        alone = left_dot(local[1], left_dot(local[0], spectrum) * inverted)
        collect(turn, used)
        jumps = []
        for which in range(2):
            total = couple[which, 0] * note_recv[turn, 0, 0:TILE]
            for source in range(1, peers):
                total = total + couple[which, source] * note_recv[turn, source, 0:TILE]
            jumps.append(as_row(total[:quarter] + total[quarter:]))
        below, above = jumps
        solved = alone - from_end * below + from_top * above
        padded = jnp.concatenate(
            [
                jnp.broadcast_to(solved[0:1] + above, (TILE, length)),
                solved,
                jnp.broadcast_to(solved[rows - 1 :] - below, (TILE, length)),
            ],
            axis=0,
        )
        return basis_dot(padded, inverse_parts)

    z0 = precondition(0, right_side, [])
    z0_mid = z0[TILE : TILE + rows]
    w0 = operator(z0)
    y0 = precondition(1, w0, [right_side * z0_mid, z0_mid * w0])
    rho0, energy0 = totals(1, 1, 2)
    alpha0 = rho0 / energy0
    r1 = right_side - alpha0 * w0
    z1 = z0 - alpha0 * y0
    z1_mid = z1[TILE : TILE + rows]
    q1 = operator(z1)
    collect(2, share(2, [fold(r1 * z1_mid), fold(z1_mid * q1), fold(z0_mid * q1)]))
    rho1, energy1, cross = totals(2, 0, 3)
    beta = rho1 / rho0
    alpha1 = rho1 / (energy1 + 2.0 * beta * cross + beta * beta * energy0)
    answer = alpha0 * z0_mid + alpha1 * (z1_mid + beta * z0_mid)
    left = r1 - alpha1 * (q1 + beta * w0)
    out_ref[0] = jnp.where(core == 0, answer[:, :cols], answer[:, cols:])
    out_ref[1] = jnp.where(core == 0, left[:, :cols], left[:, cols:])

    settle(place_send.at[pl.ds(0, last)], place_sems.at[0])
    settle(slot_send.at[:, pl.ds(0, last)], slot_send_sem)
    settle(weight.at[:, own_lanes], edge_sems.at[4])
    settle(fields.at[:, pl.ds(0, tiles)], gamma_send_sem)
    settle(note_recv.at[0, pl.ds(0, last), top], note_sems.at[0, 0])
    settle(note_recv.at[1, pl.ds(0, last)], note_sems.at[1, 0])
    settle(note_recv.at[2, pl.ds(0, last)], note_sems.at[2, 0])

    @pl.when(me > 0)
    def _():
        settle(weight.at[first_tile, own_lanes], edge_sems.at[0])
        settle(grid_out.at[:, head], seam_send_sems.at[0])

    @pl.when(me > 1)
    def _():
        settle(grid_out.at[:, top], seam_send_sems.at[1])

    @pl.when(me < last)
    def _():
        settle(weight.at[final_tile, own_lanes], edge_sems.at[2])
        settle(grid_out.at[:, tail], seam_send_sems.at[2])


def fits_kernel(peers, cores, rows, cols):
    length = rows * peers
    capacity = max(2, 2 * rows // peers)
    return (
        cores == 2
        and rows == 64
        and length == cols * cores
        and length == 4 * LANES
        and peers * capacity == LANES
        and peers == TILE
    )


def dct_matrix(length):
    freq = np.arange(length)
    angle = (2 * freq[None, :] + 1) * freq[:, None] % (4 * length)
    scale = np.sqrt(np.where(freq == 0, 1.0, 2.0) / length)
    return scale[:, None] * np.cos(angle * (math.pi / (2.0 * length)))


def exact_eigenvalues(length):
    return 4.0 * np.sin(np.arange(length) * (math.pi / (2.0 * length))) ** 2


def bf16_parts(matrix):
    parts, rest = [], matrix
    for _ in range(3):
        parts.append(rest.astype(jnp.bfloat16))
        rest = rest - parts[-1].astype(np.float64)
    return parts


def left_parts(matrix):
    first, second, third = bf16_parts(matrix)
    return np.concatenate([first, second, third, first, second, first], axis=1)


def solve_tables(peers, rows, length, damping):
    small = dct_matrix(rows)
    shift = exact_eigenvalues(length) + damping
    inverted = 1.0 / (exact_eigenvalues(rows)[:, None] + shift[None, :])
    from_top = small.T @ (small[:, 0:1] * inverted)
    near, far = from_top[0], from_top[-1]
    count = peers - 1
    system = np.zeros((length, count, count))
    for index in range(count):
        system[:, index, index] = 1.0 + 2.0 * near
        if index:
            system[:, index, index - 1] = -far
            system[:, index - 1, index] = -far
    solved = np.linalg.inv(system)
    couple = np.zeros((peers, peers, 2, length))
    for jump in range(count):
        for index in range(count):
            couple[jump, index, 1] += solved[:, jump, index]
            couple[jump, index + 1, 0] -= solved[:, jump, index]
    tables = np.stack([from_top, from_top[::-1], inverted]).astype(np.float32)
    couple = couple.reshape(peers, peers, 2 * length // LANES, LANES).astype(np.float32)
    return np.stack([left_parts(small), left_parts(small.T)]), tables, couple


def unwrap_in_kernel(reference_slc, secondary_slc, line_target, seam_partner, mask_level, peers):
    rows, cols = mask_level.shape
    length = rows * peers
    capacity = max(2, 2 * rows // peers)
    slots = peers * capacity
    damping = 0.25 / (rows * rows)
    basis = dct_matrix(length)
    inverse = np.stack(bf16_parts(basis))
    forward = np.stack(bf16_parts(basis.T))
    local, tables, couple = solve_tables(peers, rows, length, damping)
    width = reference_slc.shape[2] // PIECES
    lines = reference_slc.shape[1]
    group = (np.arange(width)[:, None] // LOOK_RG == np.arange(LANES)[None, :]).astype(jnp.bfloat16)
    hbm = pl.BlockSpec(memory_space=pl.ANY)
    vmem = pl.BlockSpec(memory_space=pltpu.VMEM)
    dma = pltpu.SemaphoreType.DMA

    def scratch(*dims):
        return pltpu.VMEM(dims, jnp.float32)

    def like(array):
        return pltpu.VMEM(array.shape, array.dtype)

    target, seam = line_target.reshape(1, rows), seam_partner.reshape(1, rows)
    both = pl.pallas_call(
        functools.partial(unwrap_kernel, peers, capacity, damping),
        out_shape=pltpu.VMEM((2, rows, cols), jnp.float32),
        in_specs=[hbm] * 11,
        out_specs=vmem,
        scratch_shapes=[
            pltpu.VMEM((PIECES, 2, 2, lines, width), jnp.bfloat16),
            like(group),
            like(target),
            like(seam),
            like(mask_level),
            like(forward),
            like(inverse),
            like(local),
            like(tables),
            scratch(2, peers, TILE, LANES),
            scratch(width // LANES * (lines // LINES), 4 * LINES, LANES),
            scratch(peers, TILE, slots),
            scratch(peers, TILE, slots),
            scratch(PIECES, peers, capacity, LANES),
            scratch(PIECES, peers, capacity, LANES),
            scratch(PIECES, 2 * rows, LANES),
            scratch(PIECES, rows + 3 * TILE, LANES),
            scratch(rows + 2 * TILE, length),
            scratch(2, length // LANES, rows + 2 * TILE, LANES),
            scratch(3, 3 * TILE, LANES),
            scratch(3, peers, 3 * TILE, LANES),
            dma((PIECES,)),
            dma((10,)),
            dma((2,)),
            dma,
            dma((PIECES,)),
            dma((3,)),
            dma((PIECES,)),
            dma((6,)),
            dma,
            dma((cols // LANES,)),
            dma((3, 2)),
        ],
        compiler_params=pltpu.CompilerParams(
            collective_id=0, has_side_effects=True, vmem_limit_bytes=63 * 2**20
        ),
        name="unwrap",
    )(
        reference_slc,
        secondary_slc,
        group,
        target,
        seam,
        mask_level,
        forward,
        inverse,
        local,
        tables,
        couple,
    )
    return both[0], both[1]


def pick_rows(wanted, stack):
    choose = (wanted[:, None] == jnp.arange(stack.shape[1], dtype=jnp.int32)).astype(jnp.float32)
    return jnp.einsum("sr,prc->psc", choose, stack, precision=FULL_PRECISION)


def single_product(left, right):
    return lax.psum(jnp.sum(left * right), ("az", "rg"))


def on_device(reference_slc, secondary_slc, line_target, seam_partner, mask_level):
    dev_count = lax.axis_size("az")
    rg_count = lax.axis_size("rg")
    az_place = lax.axis_index("az")
    rg_place = lax.axis_index("rg")
    row_count = line_target.shape[0]
    col_count = mask_level.shape[1]
    if fits_kernel(dev_count, rg_count, row_count, col_count):
        return unwrap_in_kernel(
            reference_slc, secondary_slc, line_target, seam_partner, mask_level, dev_count
        )
    local_sums = form_looks(reference_slc, secondary_slc, col_count)
    capacity = max(2, 2 * row_count // dev_count)
    owners = line_target // row_count
    local_index = jnp.arange(row_count, dtype=jnp.int32)
    earlier = (owners[:, None] == owners[None, :]) & (local_index[None, :] < local_index[:, None])
    slot_rank = jnp.sum(earlier.astype(jnp.int32), axis=1)
    slot_index = owners * capacity + slot_rank
    buffer_length = dev_count * capacity
    source_row = jnp.full((buffer_length,), row_count, jnp.int32).at[slot_index].set(local_index)
    positions = (
        jnp.full((1, buffer_length), row_count, jnp.int32)
        .at[0, slot_index]
        .set(line_target % row_count)
    )
    sent_sums = pick_rows(source_row, local_sums)
    got_sums, got_positions = (
        lax.all_to_all(sent_sums, "az", split_axis=1, concat_axis=1, tiled=True),
        lax.all_to_all(positions, "az", split_axis=1, concat_axis=1, tiled=True),
    )
    gridded = jnp.zeros_like(local_sums).at[:, got_positions[0]].set(got_sums, mode="drop")
    next_block = from_behind(gridded, "az", -1)
    combined = gridded + pick_rows(seam_partner, next_block)
    magnitude = jnp.sqrt(combined[2] * combined[3]) + EPSILON
    weight = (1 + mask_level).astype(jnp.float32) * 0.25
    fields = jnp.stack([combined[0] / magnitude, combined[1] / magnitude, weight])
    padded = with_halo(fields, (("az", 1), ("rg", 2)), 1)
    beside_all = neighbours(padded)
    edge_weights = [weight * item[2] for item in beside_all]
    right_side = jnp.zeros((row_count, col_count), jnp.float32)
    for edge, item in zip(edge_weights, beside_all):
        right_side = right_side + edge * (fields[1] * item[0] - fields[0] * item[1])
    damping = 0.25 / (row_count * row_count)
    grid_rows = row_count * dev_count
    grid_cols = col_count * rg_count
    my_cols = rg_place * col_count + jnp.arange(col_count, dtype=jnp.int32)
    column_width = col_count // dev_count
    all_rows = jnp.arange(grid_rows, dtype=jnp.int32)
    full_basis = dct_table(all_rows, all_rows, grid_rows)
    pencil_cols = (
        rg_place * col_count + az_place * column_width + jnp.arange(column_width, dtype=jnp.int32)
    )
    pencil_divisor = (
        eigenvalues(pencil_cols, grid_cols)[:, None]
        + eigenvalues(all_rows, grid_rows)[None, :]
        + damping
    )

    def precondition(values):
        basis_block = dct_table(
            jnp.arange(col_count * lax.axis_size("rg"), dtype=jnp.int32), my_cols, grid_cols
        )
        range_spectrum = lax.psum_scatter(
            contract(basis_block, values, 1, 1), "rg", scatter_dimension=0, tiled=True
        )
        pencil = lax.all_to_all(range_spectrum, "az", split_axis=0, concat_axis=1, tiled=True)
        filtered = contract(pencil, full_basis, 1, 1) / pencil_divisor
        restored = contract(filtered, full_basis, 1, 0)
        back_columns = lax.all_to_all(restored, "az", split_axis=1, concat_axis=0, tiled=True)
        basis_block = dct_table(
            my_cols, jnp.arange(col_count * lax.axis_size("rg"), dtype=jnp.int32), grid_cols
        )
        return lax.psum_scatter(
            contract(basis_block, back_columns, 0, 0), "rg", scatter_dimension=0, tiled=True
        ).T

    solution = jnp.zeros((row_count, col_count), jnp.float32)
    residual = right_side
    precond = precondition(residual)
    direction = precond
    inner_now = single_product(residual, precond)
    for turn_index in range(ITERS):
        rim = with_halo(direction, (("az", 0), ("rg", 1)), 1)
        result_sum = damping * direction
        for apply_edge, apply_item in zip(edge_weights, neighbours(rim)):
            result_sum = result_sum + apply_edge * (direction - apply_item)
        step_size = inner_now / lax.psum(jnp.sum(direction * result_sum), ("az", "rg"))
        solution = solution + step_size * direction
        residual = residual - step_size * result_sum
        if turn_index + 1 < ITERS:
            precond = precondition(residual)
            inner_next = single_product(residual, precond)
            direction = precond + inner_next / inner_now * direction
            inner_now = inner_next
    return (solution, residual)


def solution(mesh):
    in_specs = (
        P(None, ("pass", "az"), "rg"),
        P(None, ("pass", "az"), "rg"),
        P(("pass", "az")),
        P(("pass", "az")),
        P(("pass", "az"), "rg"),
    )
    out_specs = (P(("pass", "az"), "rg"), P(("pass", "az"), "rg"))
    return jax.shard_map(
        on_device, mesh=mesh, in_specs=in_specs, out_specs=out_specs, check_vma=False
    )
```

```python
import functools
import math

import jax
import jax.numpy as jnp
import numpy as np
from jax import lax
from jax.experimental import pallas as pl
from jax.experimental.pallas import tpu as pltpu
from jax.sharding import PartitionSpec as P

LOOK_AZ = 4
LOOK_RG = 20
ITERS = 2


FULL_PRECISION = lax.Precision.HIGHEST
EPSILON = 1e-06


def from_behind(value, axis, steps):
    count = lax.axis_size(axis)
    first, last = (max(0, -steps), min(count, count - steps))
    return lax.ppermute(value, axis, [(source, source + steps) for source in range(first, last)])


def with_halo(shard, sides, width):
    for axis, dim in sides:
        peers, length = (lax.axis_size(axis), shard.shape[dim])
        up = [(i, (i + 1) % peers) for i in range(peers - 1)]
        down = [(j, i) for i, j in up]
        last = lax.slice_in_dim(shard, length - width, length, axis=dim)
        first = lax.slice_in_dim(shard, 0, width, axis=dim)
        before = lax.ppermute(last, axis, up)
        after = lax.ppermute(first, axis, down)
        shard = jnp.concatenate([before, shard, after], axis=dim)
    return shard


def dct_table(freq_index, place_index, length):
    product = (2 * place_index[None, :] + 1) * freq_index[:, None] % (4 * length)
    norm_factor = jnp.where(
        freq_index == 0, math.sqrt(1.0 / length), math.sqrt(2.0 / length)
    ).astype(jnp.float32)
    return norm_factor[:, None] * jnp.cos(product.astype(jnp.float32) * (math.pi / (2.0 * length)))


def eigenvalues(freq_index, length):
    return 4.0 * jnp.sin(freq_index.astype(jnp.float32) * (math.pi / (2.0 * length))) ** 2


def neighbours(padded):
    return (
        padded[..., :-2, 1:-1],
        padded[..., 2:, 1:-1],
        padded[..., 1:-1, :-2],
        padded[..., 1:-1, 2:],
    )


def contract(left, right, left_dim, right_dim):
    return lax.dot_general(
        left,
        right,
        (((left_dim,), (right_dim,)), ((), ())),
        precision=FULL_PRECISION,
        preferred_element_type=jnp.float32,
    )


CHUNK = 256


def look_kernel(lines, half, ref_ref, sec_ref, group_ref, line_ref, out_ref):
    step_rows = lines // LOOK_AZ
    width = half // LOOK_RG
    for side in range(out_ref.shape[2] // width):
        total = jnp.zeros((8 * lines, width), jnp.float32)
        for start in range(0, half, CHUNK):
            span = pl.ds(side * half + start, CHUNK)
            mr = ref_ref[0, :, span].astype(jnp.float32)
            mi = ref_ref[1, :, span].astype(jnp.float32)
            sr = sec_ref[0, :, span].astype(jnp.float32)
            si = sec_ref[1, :, span].astype(jnp.float32)
            planes = jnp.concatenate(
                [mr * sr + mi * si, mi * sr - mr * si, mr * mr + mi * mi, sr * sr + si * si], axis=0
            )
            high = planes.astype(jnp.bfloat16)
            low = (planes - high.astype(jnp.float32)).astype(jnp.bfloat16)
            total = total + jnp.dot(
                jnp.concatenate([high, low], axis=0),
                group_ref[pl.ds(start, CHUNK), :],
                preferred_element_type=jnp.float32,
            )
        joined = total[: 4 * lines] + total[4 * lines :]
        sums = jnp.dot(
            line_ref[...], joined, precision=FULL_PRECISION, preferred_element_type=jnp.float32
        )
        for plane in range(4):
            out_ref[plane, :, side * width : (side + 1) * width] = sums[
                plane * step_rows : (plane + 1) * step_rows
            ]


def form_looks(ref_lines, sec_lines, col_count):
    line_count, sample_count = ref_lines.shape[1:]
    lines = 32
    half = 128 * LOOK_RG
    group = (np.arange(half)[:, None] // LOOK_RG == np.arange(128)[None, :]).astype(jnp.bfloat16)
    line_of = (np.arange(4 * lines)[None, :] // LOOK_AZ == np.arange(lines)[:, None]).astype(
        np.float32
    )
    block = pl.BlockSpec((2, lines, sample_count), lambda i: (0, i, 0))
    return pl.pallas_call(
        functools.partial(look_kernel, lines, half),
        grid=(line_count // lines,),
        in_specs=[
            block,
            block,
            pl.BlockSpec(group.shape, lambda i: (0, 0)),
            pl.BlockSpec(line_of.shape, lambda i: (0, 0)),
        ],
        out_specs=pl.BlockSpec((4, lines // LOOK_AZ, col_count), lambda i: (0, i, 0)),
        out_shape=jax.ShapeDtypeStruct((4, line_count // LOOK_AZ, col_count), jnp.float32),
        name="form_looks",
    )(ref_lines, sec_lines, group, line_of)


def iota(shape, dim):
    return lax.broadcasted_iota(jnp.int32, shape, dim)


def split(values):
    high = values.astype(jnp.bfloat16)
    rest = values - high.astype(jnp.float32)
    middle = rest.astype(jnp.bfloat16)
    return high, middle, (rest - middle.astype(jnp.float32)).astype(jnp.bfloat16)


def narrow_dot(left, right):
    return jnp.dot(left, right, preferred_element_type=jnp.float32)


def pick_dot(choose_thrice, values):
    return narrow_dot(choose_thrice, jnp.concatenate(split(values), axis=0))


def left_dot(parts, values):
    high, middle, low = split(values)
    return narrow_dot(parts, jnp.concatenate([low, middle, high, middle, high, high], axis=0))


def basis_dot(values, basis):
    count = values.shape[0]
    high, middle, low = split(values)
    first = narrow_dot(jnp.concatenate([high, middle, low], axis=0), basis[0])
    second = narrow_dot(jnp.concatenate([high, middle], axis=0), basis[1])
    third = narrow_dot(high, basis[2])
    small = first[2 * count :] + second[count:] + third
    return first[:count] + ((first[count : 2 * count] + second[:count]) + small)


LINES = 64
PIECES = 4
PART = 64
WIDE = 4 * PART
LAG = 4
LANES = 128
TILE = 8


def form_piece(piece, held, group, hold):
    lines_held, width = held.shape[3:]
    blocks = lines_held // LINES
    looks = LINES // LOOK_AZ
    tall = 4 * looks * blocks
    total = jnp.zeros((2 * tall, LANES), jnp.float32)
    for start in range(0, width, CHUNK):
        end = min(start + CHUNK, width)
        highs, lows = [], []
        for block in range(blocks):
            parts = []
            for begin in range(start, end, LANES):
                span = pl.ds(begin, LANES)
                lines = pl.ds(block * LINES, LINES)
                slot = begin // LANES * blocks + block
                mr = held[piece, 0, 0, lines, span].astype(jnp.float32)
                mi = held[piece, 0, 1, lines, span].astype(jnp.float32)
                sr = held[piece, 1, 0, lines, span].astype(jnp.float32)
                si = held[piece, 1, 1, lines, span].astype(jnp.float32)
                hold[slot, 0:LINES] = mr * sr + mi * si
                hold[slot, LINES : 2 * LINES] = mi * sr - mr * si
                hold[slot, 2 * LINES : 3 * LINES] = mr * mr + mi * mi
                hold[slot, 3 * LINES :] = sr * sr + si * si
                part = hold[slot, pl.ds(0, 4 * looks, stride=LOOK_AZ), :]
                for line in range(1, LOOK_AZ):
                    part = part + hold[slot, pl.ds(line, 4 * looks, stride=LOOK_AZ), :]
                parts.append(part)
            sums = jnp.concatenate(parts, axis=1)
            high = sums.astype(jnp.bfloat16)
            highs.append(high)
            lows.append((sums - high.astype(jnp.float32)).astype(jnp.bfloat16))
        total = total + narrow_dot(
            jnp.concatenate(highs + lows, axis=0), group[start:end, :]
        )
    joined = total[:tall] + total[tall:]
    planes = [
        jnp.concatenate(
            [
                joined[(4 * block + plane) * looks : (4 * block + plane + 1) * looks]
                for block in range(blocks)
            ],
            axis=0,
        )
        for plane in range(4)
    ]
    return jnp.concatenate(
        [planes[0] + pltpu.roll(planes[1], PART, 1), planes[2] + pltpu.roll(planes[3], PART, 1)],
        axis=1,
    )


def unwrap_kernel(
    peers,
    capacity,
    damping,
    ref_ref,
    sec_ref,
    group_ref,
    target_ref,
    seam_ref,
    mask_ref,
    forward_ref,
    inverse_ref,
    local_ref,
    table_ref,
    couple_ref,
    out_ref,
    held,
    group,
    target,
    seam,
    mask,
    forward,
    inverse,
    local,
    table,
    couple,
    hold,
    place_send,
    place_recv,
    slot_send,
    slot_recv,
    grid_out,
    seam_recv,
    weight,
    fields,
    note_send,
    note_recv,
    load_sems,
    table_sems,
    place_sems,
    slot_send_sem,
    slot_sems,
    seam_send_sems,
    seam_sems,
    edge_sems,
    gamma_send_sem,
    gamma_sems,
    note_sems,
):
    me = lax.axis_index("az")
    core = lax.axis_index("rg")
    other = 1 - core
    last = peers - 1
    rows, cols = mask.shape
    length = forward.shape[1]
    slots = peers * capacity
    ends = rows + 2 * TILE
    after, beyond, before = pl.ds(0, rows + TILE), pl.ds(rows + TILE, TILE), pl.ds(ends, TILE)
    piece_width = held.shape[4]

    def at(az, rg):
        return (lax.axis_index("pass"), az, rg)

    def ahead(offset):
        return lax.rem(me + offset, peers)

    def behind(offset):
        return lax.rem(me + peers - offset, peers)

    def facing(offset):
        peer = me
        bit = 1
        while bit < peers:
            if offset & bit:
                peer = peer + bit - 2 * bit * (me // bit % 2)
            bit *= 2
        return peer

    def send(source, place, device, send_sem, recv_sem):
        pltpu.make_async_remote_copy(
            src_ref=source,
            dst_ref=place,
            send_sem=send_sem,
            recv_sem=recv_sem,
            device_id=device,
            device_id_type=pl.DeviceIdType.MESH,
        ).start()

    def settle(ref, sem):
        pltpu.make_async_copy(ref, ref, sem).wait()

    barrier = pltpu.get_barrier_semaphore()
    for offset in range(peers - 1, -1, -1):
        pl.semaphore_signal(
            barrier,
            inc=1,
            device_id=at(facing(offset), core if offset else other),
            device_id_type=pl.DeviceIdType.MESH,
        )

    index_loads = [
        pltpu.make_async_copy(source, held, table_sems.at[number])
        for number, (source, held) in enumerate(
            ((target_ref, target), (seam_ref, seam), (mask_ref, mask), (group_ref, group))
        )
    ]
    for load in index_loads:
        load.start()
    for piece in range(PIECES):
        for which, source in enumerate((ref_ref, sec_ref)):
            pltpu.make_async_copy(
                source.at[:, :, pl.ds(piece * piece_width, piece_width)],
                held.at[piece, which],
                load_sems.at[piece],
            ).start()
    table_loads = [
        pltpu.make_async_copy(source, held, table_sems.at[4 + number])
        for number, (source, held) in enumerate(
            (
                (forward_ref, forward),
                (inverse_ref, inverse),
                (local_ref, local),
                (table_ref, table),
                (couple_ref.at[me], couple.at[0]),
                (couple_ref.at[behind(1)], couple.at[1]),
            )
        )
    ]
    for load in table_loads:
        load.start()

    def upright(line):
        diagonal = iota((rows, rows), 0) == iota((rows, rows), 1)
        return jnp.sum(jnp.where(diagonal, line, 0), axis=1, keepdims=True)

    for load in index_loads:
        load.wait()
    target_row = target[...]
    target_col = upright(target_row)
    owner_row = target_row // rows
    owner_col = target_col // rows
    same = owner_col == owner_row
    low_index = iota((rows, rows), 0)
    high_index = iota((rows, rows), 1)
    rank_row = jnp.sum(
        jnp.where(same & (low_index < high_index), 1, 0), axis=0, keepdims=True
    )
    rank_col = jnp.sum(
        jnp.where(same & (high_index < low_index), 1, 0), axis=1, keepdims=True
    )
    choose = jnp.where(
        iota((slots, rows), 0) == owner_row * capacity + rank_row, 1.0, 0.0
    ).astype(jnp.bfloat16)
    choose = jnp.concatenate([choose] * 3, axis=1)
    own_lanes = pl.ds(pl.multiple_of(core * cols, cols), cols)
    weight[TILE : TILE + rows, own_lanes] = (1 + mask[...]).astype(jnp.float32) * 0.25

    @pl.when(me == 0)
    def _():
        weight[0:TILE, own_lanes] = jnp.zeros((TILE, cols), jnp.float32)
        seam_recv[:, before] = jnp.zeros((PIECES, TILE, WIDE), jnp.float32)

    @pl.when(me == last)
    def _():
        weight[TILE + rows :, own_lanes] = jnp.zeros((TILE, cols), jnp.float32)
        seam_recv[:, after] = jnp.zeros((PIECES, rows + TILE, WIDE), jnp.float32)

    @pl.when(me >= last - 1)
    def _():
        seam_recv[:, beyond] = jnp.zeros((PIECES, TILE, WIDE), jnp.float32)

    def fill_places():
        place = (target_col - owner_col * rows + 1).astype(jnp.float32)
        lane = iota((rows, slots), 1)
        here = lane == me * capacity + rank_col
        seam_row = seam[...]
        seam_col = upright(jnp.where(seam_row >= 0, seam_row + 1, -1)).astype(jnp.float32)
        seam_line = jnp.sum(jnp.where(lane == iota((rows, slots), 0), seam_col, 0.0), axis=0, keepdims=True)
        for dest in range(peers):
            line = jnp.sum(
                jnp.where(here & (owner_col == dest), place, 0.0), axis=0, keepdims=True
            )
            place_send[dest] = jnp.where(iota((TILE, slots), 0) == 0, line, seam_line)

    first_tile, final_tile = pl.ds(TILE, TILE), pl.ds(rows, TILE)
    above_tile, below_tile = pl.ds(0, TILE), pl.ds(TILE + rows, TILE)

    def send_slots(piece):
        settle(held.at[piece], load_sems.at[piece])
        looks = form_piece(piece, held, group, hold)
        slot_send[piece] = pick_dot(choose, looks).reshape(peers, capacity, WIDE)
        if piece == 0:
            pl.semaphore_wait(barrier, peers)
        for offset in range(peers - 1, 0, -1):
            send(
                slot_send.at[piece, facing(offset)],
                slot_recv.at[piece, me],
                at(facing(offset), core),
                slot_send_sem,
                slot_sems.at[piece],
            )
        slot_recv[piece, me] = slot_send[piece, me]
        if piece == 0:
            fill_places()
            for offset in range(peers - 1, 0, -1):
                send(
                    place_send.at[facing(offset)],
                    place_recv.at[me],
                    at(facing(offset), core),
                    place_sems.at[0],
                    place_sems.at[1],
                )
            place_recv[me] = place_send[me]

    for piece in range(PIECES):
        send_slots(piece)

    @pl.when(me > 0)
    def _():
        send(
            weight.at[first_tile, own_lanes],
            weight.at[below_tile, own_lanes],
            at(behind(1), core),
            edge_sems.at[0],
            edge_sems.at[1],
        )

    @pl.when(me < last)
    def _():
        send(
            weight.at[final_tile, own_lanes],
            weight.at[above_tile, own_lanes],
            at(ahead(1), core),
            edge_sems.at[2],
            edge_sems.at[3],
        )

    settle(place_recv.at[pl.ds(0, last)], place_sems.at[1])
    places = place_recv[0][0:1]
    for source in range(1, peers):
        places = places + place_recv[source][0:1]
    seam_wanted = upright(place_recv[behind(1)][1:2, :rows])
    own_wanted = (iota((rows, slots), 0) + 1).astype(jnp.float32)
    scatter = jnp.concatenate(
        [
            jnp.where(places == seam_wanted, 1.0, 0.0),
            jnp.where(places == own_wanted, 1.0, 0.0),
        ],
        axis=0,
    ).astype(jnp.bfloat16)
    scatter = jnp.concatenate([scatter] * 3, axis=1)

    @pl.when(me < last)
    def _():
        settle(weight.at[below_tile, own_lanes], edge_sems.at[1])

    @pl.when(me > 0)
    def _():
        settle(weight.at[above_tile, own_lanes], edge_sems.at[3])

    send(
        weight.at[:, own_lanes],
        weight.at[:, own_lanes],
        at(me, other),
        edge_sems.at[4],
        edge_sems.at[5],
    )
    head = pl.ds(0, rows + TILE)
    top = pl.ds(0, TILE)
    tail = pl.ds(2 * rows - TILE, TILE)

    def send_seams(piece):
        settle(slot_recv.at[piece, pl.ds(0, last)], slot_sems.at[piece])
        arrived = slot_recv[piece].reshape(slots, WIDE)
        grid_out[piece] = pick_dot(scatter, arrived)

        @pl.when(me > 0)
        def _():
            send(
                grid_out.at[piece, head],
                seam_recv.at[piece, after],
                at(behind(1), core),
                seam_send_sems.at[0],
                seam_sems.at[piece],
            )

        @pl.when(me > 1)
        def _():
            send(
                grid_out.at[piece, top],
                seam_recv.at[piece, beyond],
                at(behind(2), core),
                seam_send_sems.at[1],
                seam_sems.at[piece],
            )

        @pl.when(me < last)
        def _():
            send(
                grid_out.at[piece, tail],
                seam_recv.at[piece, before],
                at(ahead(1), core),
                seam_send_sems.at[2],
                seam_sems.at[piece],
            )

    part_of = iota((ends, LANES), 1) // PART

    def send_gamma(piece, planes):
        @pl.when((me > 0) & (me < last - 1))
        def _():
            settle(seam_recv.at[piece], seam_sems.at[piece])

        @pl.when((me == 0) | (me == last - 1))
        def _():
            settle(seam_recv.at[piece, pl.ds(0, ends)], seam_sems.at[piece])

        @pl.when(me == last)
        def _():
            settle(seam_recv.at[piece, before], seam_sems.at[piece])

        own = grid_out[piece]
        coming = seam_recv[piece]
        combined = jnp.concatenate(
            [
                coming[ends:] + own[rows - TILE : rows],
                own[rows:] + coming[:rows],
                coming[rows : rows + TILE] + coming[rows + TILE : ends],
            ],
            axis=0,
        )
        powers = combined[:, LANES:]
        gamma = combined[:, :LANES] / (jnp.sqrt(powers * pltpu.roll(powers, PART, 1)) + EPSILON)
        tile, spot = piece * PART // LANES, piece % (LANES // PART)
        for plane in range(2):
            moved = (spot - plane) * PART % LANES
            part = pltpu.roll(gamma, moved, 1) if moved else gamma
            planes[plane] = jnp.where(part_of == spot, part, planes[plane]) if spot else part
        if spot == LANES // PART - 1:
            place = core * (cols // LANES) + tile
            for plane in range(2):
                fields[plane, place] = planes[plane]
            send(
                fields.at[:, place],
                fields.at[:, place],
                at(me, other),
                gamma_send_sem,
                gamma_sems.at[tile],
            )

    planes = [None, None]
    for piece in range(PIECES + LAG):
        if piece < PIECES:
            send_seams(piece)
        if piece >= LAG:
            send_gamma(piece - LAG, planes)
    for load in table_loads:
        load.wait()
    settle(weight.at[:, own_lanes], edge_sems.at[5])

    column = iota((rows, length), 1)

    def beside(values):
        middle = values[TILE : TILE + rows]
        return (
            values[TILE - 1 : TILE - 1 + rows],
            values[TILE + 1 : TILE + 1 + rows],
            pltpu.roll(middle, 1, 1),
            pltpu.roll(middle, length - 1, 1),
        )

    weights = weight[...]
    inside = weights[TILE : TILE + rows]
    edges = [inside * item for item in beside(weights)]
    edges[2] = jnp.where(column > 0, edges[2], 0.0)
    edges[3] = jnp.where(column < length - 1, edges[3], 0.0)
    tiles = cols // LANES
    for tile in range(tiles):
        settle(fields.at[:, tile], gamma_sems.at[tile])
    real, imag = [
        jnp.concatenate([fields[plane, tile] for tile in range(2 * tiles)], axis=1)
        for plane in range(2)
    ]
    right_side = jnp.zeros((rows, length), jnp.float32)
    for edge, real_item, imag_item in zip(edges, beside(real), beside(imag)):
        right_side = right_side + edge * (
            imag[TILE : TILE + rows] * real_item - real[TILE : TILE + rows] * imag_item
        )

    def operator(values):
        middle = values[TILE : TILE + rows]
        result = damping * middle
        for edge, item in zip(edges, beside(values)):
            result = result + edge * (middle - item)
        return result

    def fold(values):
        total = None
        for row in range(0, rows, TILE):
            for begin in range(0, length, LANES):
                part = values[row : row + TILE, begin : begin + LANES]
                total = part if total is None else total + part
        return total

    def share(turn, tiles):
        for index, tile in enumerate(tiles):
            note_send[turn, index * TILE : (index + 1) * TILE] = tile
        used = pl.ds(0, len(tiles) * TILE)
        for offset in range(peers - 1, 0, -1):
            send(
                note_send.at[turn, used],
                note_recv.at[turn, me, used],
                at(facing(offset), core),
                note_sems.at[turn, 0],
                note_sems.at[turn, 1],
            )
        note_recv[turn, me, used] = note_send[turn, used]
        return used

    def collect(turn, used):
        settle(note_recv.at[turn, pl.ds(0, last), used], note_sems.at[turn, 1])

    def totals(turn, first, count):
        results = []
        for index in range(first, first + count):
            total = note_recv[turn, 0, index * TILE : (index + 1) * TILE]
            for source in range(1, peers):
                total = total + note_recv[turn, source, index * TILE : (index + 1) * TILE]
            results.append(jnp.sum(total, keepdims=True))
        return results

    forward_parts = [forward[part] for part in range(3)]
    inverse_parts = [inverse[part] for part in range(3)]
    quarter = length // LANES

    def as_row(tile):
        return jnp.concatenate([tile[index : index + 1] for index in range(quarter)], axis=1)

    def precondition(turn, values, products):
        spectrum = basis_dot(values, forward_parts)
        from_top, from_end, inverted = table[0], table[1], table[2]
        first = jnp.sum(spectrum * from_top, axis=0, keepdims=True)
        final = jnp.sum(spectrum * from_end, axis=0, keepdims=True)
        rims = jnp.concatenate(
            [
                line[:, begin : begin + LANES]
                for line in (first, final)
                for begin in range(0, length, LANES)
            ],
            axis=0,
        )
        used = share(turn, [rims] + [fold(product) for product in products])
        alone = left_dot(local[1], left_dot(local[0], spectrum) * inverted)
        collect(turn, used)
        jumps = []
        for which in range(2):
            total = couple[which, 0] * note_recv[turn, 0, 0:TILE]
            for source in range(1, peers):
                total = total + couple[which, source] * note_recv[turn, source, 0:TILE]
            jumps.append(as_row(total[:quarter] + total[quarter:]))
        below, above = jumps
        solved = alone - from_end * below + from_top * above
        padded = jnp.concatenate(
            [
                jnp.broadcast_to(solved[0:1] + above, (TILE, length)),
                solved,
                jnp.broadcast_to(solved[rows - 1 :] - below, (TILE, length)),
            ],
            axis=0,
        )
        return basis_dot(padded, inverse_parts)

    z0 = precondition(0, right_side, [])
    z0_mid = z0[TILE : TILE + rows]
    w0 = operator(z0)
    y0 = precondition(1, w0, [right_side * z0_mid, z0_mid * w0])
    rho0, energy0 = totals(1, 1, 2)
    alpha0 = rho0 / energy0
    r1 = right_side - alpha0 * w0
    z1 = z0 - alpha0 * y0
    z1_mid = z1[TILE : TILE + rows]
    q1 = operator(z1)
    collect(2, share(2, [fold(r1 * z1_mid), fold(z1_mid * q1), fold(z0_mid * q1)]))
    rho1, energy1, cross = totals(2, 0, 3)
    beta = rho1 / rho0
    alpha1 = rho1 / (energy1 + 2.0 * beta * cross + beta * beta * energy0)
    answer = alpha0 * z0_mid + alpha1 * (z1_mid + beta * z0_mid)
    left = r1 - alpha1 * (q1 + beta * w0)
    out_ref[0] = jnp.where(core == 0, answer[:, :cols], answer[:, cols:])
    out_ref[1] = jnp.where(core == 0, left[:, :cols], left[:, cols:])

    settle(place_send.at[pl.ds(0, last)], place_sems.at[0])
    settle(slot_send.at[:, pl.ds(0, last)], slot_send_sem)
    settle(weight.at[:, own_lanes], edge_sems.at[4])
    settle(fields.at[:, pl.ds(0, tiles)], gamma_send_sem)
    settle(note_recv.at[0, pl.ds(0, last), top], note_sems.at[0, 0])
    settle(note_recv.at[1, pl.ds(0, last)], note_sems.at[1, 0])
    settle(note_recv.at[2, pl.ds(0, last)], note_sems.at[2, 0])

    @pl.when(me > 0)
    def _():
        settle(weight.at[first_tile, own_lanes], edge_sems.at[0])
        settle(grid_out.at[:, head], seam_send_sems.at[0])

    @pl.when(me > 1)
    def _():
        settle(grid_out.at[:, top], seam_send_sems.at[1])

    @pl.when(me < last)
    def _():
        settle(weight.at[final_tile, own_lanes], edge_sems.at[2])
        settle(grid_out.at[:, tail], seam_send_sems.at[2])


def fits_kernel(peers, cores, rows, cols):
    length = rows * peers
    capacity = max(2, 2 * rows // peers)
    return (
        cores == 2
        and rows == 64
        and length == cols * cores
        and length == 4 * LANES
        and peers * capacity == LANES
        and peers == TILE
    )


def dct_matrix(length):
    freq = np.arange(length)
    angle = (2 * freq[None, :] + 1) * freq[:, None] % (4 * length)
    scale = np.sqrt(np.where(freq == 0, 1.0, 2.0) / length)
    return scale[:, None] * np.cos(angle * (math.pi / (2.0 * length)))


def exact_eigenvalues(length):
    return 4.0 * np.sin(np.arange(length) * (math.pi / (2.0 * length))) ** 2


def bf16_parts(matrix):
    parts, rest = [], matrix
    for _ in range(3):
        parts.append(rest.astype(jnp.bfloat16))
        rest = rest - parts[-1].astype(np.float64)
    return parts


def left_parts(matrix):
    first, second, third = bf16_parts(matrix)
    return np.concatenate([first, second, third, first, second, first], axis=1)


def solve_tables(peers, rows, length, damping):
    small = dct_matrix(rows)
    shift = exact_eigenvalues(length) + damping
    inverted = 1.0 / (exact_eigenvalues(rows)[:, None] + shift[None, :])
    from_top = small.T @ (small[:, 0:1] * inverted)
    near, far = from_top[0], from_top[-1]
    count = peers - 1
    system = np.zeros((length, count, count))
    for index in range(count):
        system[:, index, index] = 1.0 + 2.0 * near
        if index:
            system[:, index, index - 1] = -far
            system[:, index - 1, index] = -far
    solved = np.linalg.inv(system)
    couple = np.zeros((peers, peers, 2, length))
    for jump in range(count):
        for index in range(count):
            couple[jump, index, 1] += solved[:, jump, index]
            couple[jump, index + 1, 0] -= solved[:, jump, index]
    tables = np.stack([from_top, from_top[::-1], inverted]).astype(np.float32)
    couple = couple.reshape(peers, peers, 2 * length // LANES, LANES).astype(np.float32)
    return np.stack([left_parts(small), left_parts(small.T)]), tables, couple


def unwrap_in_kernel(reference_slc, secondary_slc, line_target, seam_partner, mask_level, peers):
    rows, cols = mask_level.shape
    length = rows * peers
    capacity = max(2, 2 * rows // peers)
    slots = peers * capacity
    damping = 0.25 / (rows * rows)
    basis = dct_matrix(length)
    inverse = np.stack(bf16_parts(basis))
    forward = np.stack(bf16_parts(basis.T))
    local, tables, couple = solve_tables(peers, rows, length, damping)
    width = reference_slc.shape[2] // PIECES
    lines = reference_slc.shape[1]
    group = (np.arange(width)[:, None] // LOOK_RG == np.arange(LANES)[None, :]).astype(jnp.bfloat16)
    hbm = pl.BlockSpec(memory_space=pl.ANY)
    vmem = pl.BlockSpec(memory_space=pltpu.VMEM)
    dma = pltpu.SemaphoreType.DMA

    def scratch(*dims):
        return pltpu.VMEM(dims, jnp.float32)

    def like(array):
        return pltpu.VMEM(array.shape, array.dtype)

    target, seam = line_target.reshape(1, rows), seam_partner.reshape(1, rows)
    both = pl.pallas_call(
        functools.partial(unwrap_kernel, peers, capacity, damping),
        out_shape=pltpu.VMEM((2, rows, cols), jnp.float32),
        in_specs=[hbm] * 11,
        out_specs=vmem,
        scratch_shapes=[
            pltpu.VMEM((PIECES, 2, 2, lines, width), jnp.bfloat16),
            like(group),
            like(target),
            like(seam),
            like(mask_level),
            like(forward),
            like(inverse),
            like(local),
            like(tables),
            scratch(2, peers, TILE, LANES),
            scratch(width // LANES * (lines // LINES), 4 * LINES, LANES),
            scratch(peers, TILE, slots),
            scratch(peers, TILE, slots),
            scratch(PIECES, peers, capacity, WIDE),
            scratch(PIECES, peers, capacity, WIDE),
            scratch(PIECES, 2 * rows, WIDE),
            scratch(PIECES, rows + 3 * TILE, WIDE),
            scratch(rows + 2 * TILE, length),
            scratch(2, length // LANES, rows + 2 * TILE, LANES),
            scratch(3, 3 * TILE, LANES),
            scratch(3, peers, 3 * TILE, LANES),
            dma((PIECES,)),
            dma((10,)),
            dma((2,)),
            dma,
            dma((PIECES,)),
            dma((3,)),
            dma((PIECES,)),
            dma((6,)),
            dma,
            dma((cols // LANES,)),
            dma((3, 2)),
        ],
        compiler_params=pltpu.CompilerParams(
            collective_id=0, has_side_effects=True, vmem_limit_bytes=63 * 2**20
        ),
        name="unwrap",
    )(
        reference_slc,
        secondary_slc,
        group,
        target,
        seam,
        mask_level,
        forward,
        inverse,
        local,
        tables,
        couple,
    )
    return both[0], both[1]


def pick_rows(wanted, stack):
    choose = (wanted[:, None] == jnp.arange(stack.shape[1], dtype=jnp.int32)).astype(jnp.float32)
    return jnp.einsum("sr,prc->psc", choose, stack, precision=FULL_PRECISION)


def single_product(left, right):
    return lax.psum(jnp.sum(left * right), ("az", "rg"))


def on_device(reference_slc, secondary_slc, line_target, seam_partner, mask_level):
    dev_count = lax.axis_size("az")
    rg_count = lax.axis_size("rg")
    az_place = lax.axis_index("az")
    rg_place = lax.axis_index("rg")
    row_count = line_target.shape[0]
    col_count = mask_level.shape[1]
    if fits_kernel(dev_count, rg_count, row_count, col_count):
        return unwrap_in_kernel(
            reference_slc, secondary_slc, line_target, seam_partner, mask_level, dev_count
        )
    local_sums = form_looks(reference_slc, secondary_slc, col_count)
    capacity = max(2, 2 * row_count // dev_count)
    owners = line_target // row_count
    local_index = jnp.arange(row_count, dtype=jnp.int32)
    earlier = (owners[:, None] == owners[None, :]) & (local_index[None, :] < local_index[:, None])
    slot_rank = jnp.sum(earlier.astype(jnp.int32), axis=1)
    slot_index = owners * capacity + slot_rank
    buffer_length = dev_count * capacity
    source_row = jnp.full((buffer_length,), row_count, jnp.int32).at[slot_index].set(local_index)
    positions = (
        jnp.full((1, buffer_length), row_count, jnp.int32)
        .at[0, slot_index]
        .set(line_target % row_count)
    )
    sent_sums = pick_rows(source_row, local_sums)
    got_sums, got_positions = (
        lax.all_to_all(sent_sums, "az", split_axis=1, concat_axis=1, tiled=True),
        lax.all_to_all(positions, "az", split_axis=1, concat_axis=1, tiled=True),
    )
    gridded = jnp.zeros_like(local_sums).at[:, got_positions[0]].set(got_sums, mode="drop")
    next_block = from_behind(gridded, "az", -1)
    combined = gridded + pick_rows(seam_partner, next_block)
    magnitude = jnp.sqrt(combined[2] * combined[3]) + EPSILON
    weight = (1 + mask_level).astype(jnp.float32) * 0.25
    fields = jnp.stack([combined[0] / magnitude, combined[1] / magnitude, weight])
    padded = with_halo(fields, (("az", 1), ("rg", 2)), 1)
    beside_all = neighbours(padded)
    edge_weights = [weight * item[2] for item in beside_all]
    right_side = jnp.zeros((row_count, col_count), jnp.float32)
    for edge, item in zip(edge_weights, beside_all):
        right_side = right_side + edge * (fields[1] * item[0] - fields[0] * item[1])
    damping = 0.25 / (row_count * row_count)
    grid_rows = row_count * dev_count
    grid_cols = col_count * rg_count
    my_cols = rg_place * col_count + jnp.arange(col_count, dtype=jnp.int32)
    column_width = col_count // dev_count
    all_rows = jnp.arange(grid_rows, dtype=jnp.int32)
    full_basis = dct_table(all_rows, all_rows, grid_rows)
    pencil_cols = (
        rg_place * col_count + az_place * column_width + jnp.arange(column_width, dtype=jnp.int32)
    )
    pencil_divisor = (
        eigenvalues(pencil_cols, grid_cols)[:, None]
        + eigenvalues(all_rows, grid_rows)[None, :]
        + damping
    )

    def precondition(values):
        basis_block = dct_table(
            jnp.arange(col_count * lax.axis_size("rg"), dtype=jnp.int32), my_cols, grid_cols
        )
        range_spectrum = lax.psum_scatter(
            contract(basis_block, values, 1, 1), "rg", scatter_dimension=0, tiled=True
        )
        pencil = lax.all_to_all(range_spectrum, "az", split_axis=0, concat_axis=1, tiled=True)
        filtered = contract(pencil, full_basis, 1, 1) / pencil_divisor
        restored = contract(filtered, full_basis, 1, 0)
        back_columns = lax.all_to_all(restored, "az", split_axis=1, concat_axis=0, tiled=True)
        basis_block = dct_table(
            my_cols, jnp.arange(col_count * lax.axis_size("rg"), dtype=jnp.int32), grid_cols
        )
        return lax.psum_scatter(
            contract(basis_block, back_columns, 0, 0), "rg", scatter_dimension=0, tiled=True
        ).T

    solution = jnp.zeros((row_count, col_count), jnp.float32)
    residual = right_side
    precond = precondition(residual)
    direction = precond
    inner_now = single_product(residual, precond)
    for turn_index in range(ITERS):
        rim = with_halo(direction, (("az", 0), ("rg", 1)), 1)
        result_sum = damping * direction
        for apply_edge, apply_item in zip(edge_weights, neighbours(rim)):
            result_sum = result_sum + apply_edge * (direction - apply_item)
        step_size = inner_now / lax.psum(jnp.sum(direction * result_sum), ("az", "rg"))
        solution = solution + step_size * direction
        residual = residual - step_size * result_sum
        if turn_index + 1 < ITERS:
            precond = precondition(residual)
            inner_next = single_product(residual, precond)
            direction = precond + inner_next / inner_now * direction
            inner_now = inner_next
    return (solution, residual)


def solution(mesh):
    in_specs = (
        P(None, ("pass", "az"), "rg"),
        P(None, ("pass", "az"), "rg"),
        P(("pass", "az")),
        P(("pass", "az")),
        P(("pass", "az"), "rg"),
    )
    out_specs = (P(("pass", "az"), "rg"), P(("pass", "az"), "rg"))
    return jax.shard_map(
        on_device, mesh=mesh, in_specs=in_specs, out_specs=out_specs, check_vma=False
    )
```

```python
import functools
import math

import jax
import jax.numpy as jnp
import numpy as np
from jax import lax
from jax.experimental import pallas as pl
from jax.experimental.pallas import tpu as pltpu
from jax.sharding import PartitionSpec as P

LOOK_AZ = 4
LOOK_RG = 20
ITERS = 2


FULL_PRECISION = lax.Precision.HIGHEST
EPSILON = 1e-06


def from_behind(value, axis, steps):
    count = lax.axis_size(axis)
    first, last = (max(0, -steps), min(count, count - steps))
    return lax.ppermute(value, axis, [(source, source + steps) for source in range(first, last)])


def with_halo(shard, sides, width):
    for axis, dim in sides:
        peers, length = (lax.axis_size(axis), shard.shape[dim])
        up = [(i, (i + 1) % peers) for i in range(peers - 1)]
        down = [(j, i) for i, j in up]
        last = lax.slice_in_dim(shard, length - width, length, axis=dim)
        first = lax.slice_in_dim(shard, 0, width, axis=dim)
        before = lax.ppermute(last, axis, up)
        after = lax.ppermute(first, axis, down)
        shard = jnp.concatenate([before, shard, after], axis=dim)
    return shard


def dct_table(freq_index, place_index, length):
    product = (2 * place_index[None, :] + 1) * freq_index[:, None] % (4 * length)
    norm_factor = jnp.where(
        freq_index == 0, math.sqrt(1.0 / length), math.sqrt(2.0 / length)
    ).astype(jnp.float32)
    return norm_factor[:, None] * jnp.cos(product.astype(jnp.float32) * (math.pi / (2.0 * length)))


def eigenvalues(freq_index, length):
    return 4.0 * jnp.sin(freq_index.astype(jnp.float32) * (math.pi / (2.0 * length))) ** 2


def neighbours(padded):
    return (
        padded[..., :-2, 1:-1],
        padded[..., 2:, 1:-1],
        padded[..., 1:-1, :-2],
        padded[..., 1:-1, 2:],
    )


def contract(left, right, left_dim, right_dim):
    return lax.dot_general(
        left,
        right,
        (((left_dim,), (right_dim,)), ((), ())),
        precision=FULL_PRECISION,
        preferred_element_type=jnp.float32,
    )


CHUNK = 256


def look_kernel(lines, half, ref_ref, sec_ref, group_ref, line_ref, out_ref):
    step_rows = lines // LOOK_AZ
    width = half // LOOK_RG
    for side in range(out_ref.shape[2] // width):
        total = jnp.zeros((8 * lines, width), jnp.float32)
        for start in range(0, half, CHUNK):
            span = pl.ds(side * half + start, CHUNK)
            mr = ref_ref[0, :, span].astype(jnp.float32)
            mi = ref_ref[1, :, span].astype(jnp.float32)
            sr = sec_ref[0, :, span].astype(jnp.float32)
            si = sec_ref[1, :, span].astype(jnp.float32)
            planes = jnp.concatenate(
                [mr * sr + mi * si, mi * sr - mr * si, mr * mr + mi * mi, sr * sr + si * si], axis=0
            )
            high = planes.astype(jnp.bfloat16)
            low = (planes - high.astype(jnp.float32)).astype(jnp.bfloat16)
            total = total + jnp.dot(
                jnp.concatenate([high, low], axis=0),
                group_ref[pl.ds(start, CHUNK), :],
                preferred_element_type=jnp.float32,
            )
        joined = total[: 4 * lines] + total[4 * lines :]
        sums = jnp.dot(
            line_ref[...], joined, precision=FULL_PRECISION, preferred_element_type=jnp.float32
        )
        for plane in range(4):
            out_ref[plane, :, side * width : (side + 1) * width] = sums[
                plane * step_rows : (plane + 1) * step_rows
            ]


def form_looks(ref_lines, sec_lines, col_count):
    line_count, sample_count = ref_lines.shape[1:]
    lines = 32
    half = 128 * LOOK_RG
    group = (np.arange(half)[:, None] // LOOK_RG == np.arange(128)[None, :]).astype(jnp.bfloat16)
    line_of = (np.arange(4 * lines)[None, :] // LOOK_AZ == np.arange(lines)[:, None]).astype(
        np.float32
    )
    block = pl.BlockSpec((2, lines, sample_count), lambda i: (0, i, 0))
    return pl.pallas_call(
        functools.partial(look_kernel, lines, half),
        grid=(line_count // lines,),
        in_specs=[
            block,
            block,
            pl.BlockSpec(group.shape, lambda i: (0, 0)),
            pl.BlockSpec(line_of.shape, lambda i: (0, 0)),
        ],
        out_specs=pl.BlockSpec((4, lines // LOOK_AZ, col_count), lambda i: (0, i, 0)),
        out_shape=jax.ShapeDtypeStruct((4, line_count // LOOK_AZ, col_count), jnp.float32),
        name="form_looks",
    )(ref_lines, sec_lines, group, line_of)


def iota(shape, dim):
    return lax.broadcasted_iota(jnp.int32, shape, dim)


def split(values):
    high = values.astype(jnp.bfloat16)
    rest = values - high.astype(jnp.float32)
    middle = rest.astype(jnp.bfloat16)
    return high, middle, (rest - middle.astype(jnp.float32)).astype(jnp.bfloat16)


def narrow_dot(left, right):
    return jnp.dot(left, right, preferred_element_type=jnp.float32)


def pick_dot(choose_thrice, values):
    return narrow_dot(choose_thrice, jnp.concatenate(split(values), axis=0))


def left_dot(parts, values):
    high, middle, low = split(values)
    return narrow_dot(parts, jnp.concatenate([low, middle, high, middle, high, high], axis=0))


def basis_dot(values, basis):
    count = values.shape[0]
    high, middle, low = split(values)
    first = narrow_dot(jnp.concatenate([high, middle, low], axis=0), basis[0])
    second = narrow_dot(jnp.concatenate([high, middle], axis=0), basis[1])
    third = narrow_dot(high, basis[2])
    small = first[2 * count :] + second[count:] + third
    return first[:count] + ((first[count : 2 * count] + second[:count]) + small)


LINES = 64
PIECES = 4
PART = 64
WIDE = 4 * PART
LAG = 4
LANES = 128
TILE = 8


def form_piece(piece, held, group, hold):
    lines_held, width = held.shape[3:]
    blocks = lines_held // LINES
    looks = LINES // LOOK_AZ
    tall = 4 * looks * blocks
    total = jnp.zeros((2 * tall, LANES), jnp.float32)
    for start in range(0, width, CHUNK):
        end = min(start + CHUNK, width)
        highs, lows = [], []
        for block in range(blocks):
            parts = []
            for begin in range(start, end, LANES):
                span = pl.ds(begin, LANES)
                lines = pl.ds(block * LINES, LINES)
                slot = begin // LANES * blocks + block
                mr = held[piece, 0, 0, lines, span].astype(jnp.float32)
                mi = held[piece, 0, 1, lines, span].astype(jnp.float32)
                sr = held[piece, 1, 0, lines, span].astype(jnp.float32)
                si = held[piece, 1, 1, lines, span].astype(jnp.float32)
                hold[slot, 0:LINES] = mr * sr + mi * si
                hold[slot, LINES : 2 * LINES] = mi * sr - mr * si
                hold[slot, 2 * LINES : 3 * LINES] = mr * mr + mi * mi
                hold[slot, 3 * LINES :] = sr * sr + si * si
                part = hold[slot, pl.ds(0, 4 * looks, stride=LOOK_AZ), :]
                for line in range(1, LOOK_AZ):
                    part = part + hold[slot, pl.ds(line, 4 * looks, stride=LOOK_AZ), :]
                parts.append(part)
            sums = jnp.concatenate(parts, axis=1)
            high = sums.astype(jnp.bfloat16)
            highs.append(high)
            lows.append((sums - high.astype(jnp.float32)).astype(jnp.bfloat16))
        total = total + narrow_dot(
            jnp.concatenate(highs + lows, axis=0), group[start:end, :]
        )
    joined = total[:tall] + total[tall:]
    planes = [
        jnp.concatenate(
            [
                joined[(4 * block + plane) * looks : (4 * block + plane + 1) * looks]
                for block in range(blocks)
            ],
            axis=0,
        )
        for plane in range(4)
    ]
    return jnp.concatenate(
        [planes[0] + pltpu.roll(planes[1], PART, 1), planes[2] + pltpu.roll(planes[3], PART, 1)],
        axis=1,
    )


def unwrap_kernel(
    peers,
    capacity,
    damping,
    ref_ref,
    sec_ref,
    group_ref,
    target_ref,
    seam_ref,
    mask_ref,
    forward_ref,
    inverse_ref,
    local_ref,
    table_ref,
    couple_ref,
    out_ref,
    held,
    group,
    target,
    seam,
    mask,
    forward,
    inverse,
    local,
    table,
    couple,
    hold,
    place_send,
    place_recv,
    slot_send,
    slot_recv,
    grid_out,
    seam_recv,
    weight,
    fields,
    note_send,
    note_recv,
    load_sems,
    table_sems,
    place_sems,
    slot_send_sem,
    slot_sems,
    seam_send_sems,
    seam_sems,
    edge_sems,
    gamma_send_sem,
    gamma_sems,
    note_sems,
):
    me = lax.axis_index("az")
    core = lax.axis_index("rg")
    other = 1 - core
    last = peers - 1
    rows, cols = mask.shape
    length = forward.shape[1]
    slots = peers * capacity
    ends = rows + 2 * TILE
    after, beyond, before = pl.ds(0, rows + TILE), pl.ds(rows + TILE, TILE), pl.ds(ends, TILE)
    piece_width = held.shape[4]

    def at(az, rg):
        return (lax.axis_index("pass"), az, rg)

    def ahead(offset):
        return lax.rem(me + offset, peers)

    def behind(offset):
        return lax.rem(me + peers - offset, peers)

    def facing(offset):
        peer = me
        bit = 1
        while bit < peers:
            if offset & bit:
                peer = peer + bit - 2 * bit * (me // bit % 2)
            bit *= 2
        return peer

    def send(source, place, device, send_sem, recv_sem):
        pltpu.make_async_remote_copy(
            src_ref=source,
            dst_ref=place,
            send_sem=send_sem,
            recv_sem=recv_sem,
            device_id=device,
            device_id_type=pl.DeviceIdType.MESH,
        ).start()

    def settle(ref, sem):
        pltpu.make_async_copy(ref, ref, sem).wait()

    barrier = pltpu.get_barrier_semaphore()
    for offset in range(peers - 1, -1, -1):
        pl.semaphore_signal(
            barrier,
            inc=1,
            device_id=at(facing(offset), core if offset else other),
            device_id_type=pl.DeviceIdType.MESH,
        )

    index_loads = [
        pltpu.make_async_copy(source, held, table_sems.at[number])
        for number, (source, held) in enumerate(
            ((target_ref, target), (seam_ref, seam), (mask_ref, mask), (group_ref, group))
        )
    ]
    for load in index_loads:
        load.start()
    def load_piece(piece):
        for which, source in enumerate((ref_ref, sec_ref)):
            pltpu.make_async_copy(
                source.at[:, :, pl.ds(piece * piece_width, piece_width)],
                held.at[piece, which],
                load_sems.at[piece],
            ).start()
    for piece in range(1):
        load_piece(piece)
    table_loads = [
        pltpu.make_async_copy(source, held, table_sems.at[4 + number])
        for number, (source, held) in enumerate(
            (
                (forward_ref, forward),
                (inverse_ref, inverse),
                (local_ref, local),
                (table_ref, table),
                (couple_ref.at[me], couple.at[0]),
                (couple_ref.at[behind(1)], couple.at[1]),
            )
        )
    ]

    def upright(line):
        diagonal = iota((rows, rows), 0) == iota((rows, rows), 1)
        return jnp.sum(jnp.where(diagonal, line, 0), axis=1, keepdims=True)

    for load in index_loads:
        load.wait()
    target_row = target[...]
    target_col = upright(target_row)
    owner_row = target_row // rows
    owner_col = target_col // rows
    same = owner_col == owner_row
    low_index = iota((rows, rows), 0)
    high_index = iota((rows, rows), 1)
    rank_row = jnp.sum(
        jnp.where(same & (low_index < high_index), 1, 0), axis=0, keepdims=True
    )
    rank_col = jnp.sum(
        jnp.where(same & (high_index < low_index), 1, 0), axis=1, keepdims=True
    )
    choose = jnp.where(
        iota((slots, rows), 0) == owner_row * capacity + rank_row, 1.0, 0.0
    ).astype(jnp.bfloat16)
    choose = jnp.concatenate([choose] * 3, axis=1)
    own_lanes = pl.ds(pl.multiple_of(core * cols, cols), cols)
    weight[TILE : TILE + rows, own_lanes] = (1 + mask[...]).astype(jnp.float32) * 0.25

    @pl.when(me == 0)
    def _():
        weight[0:TILE, own_lanes] = jnp.zeros((TILE, cols), jnp.float32)
        seam_recv[:, before] = jnp.zeros((PIECES, TILE, WIDE), jnp.float32)

    @pl.when(me == last)
    def _():
        weight[TILE + rows :, own_lanes] = jnp.zeros((TILE, cols), jnp.float32)
        seam_recv[:, after] = jnp.zeros((PIECES, rows + TILE, WIDE), jnp.float32)

    @pl.when(me >= last - 1)
    def _():
        seam_recv[:, beyond] = jnp.zeros((PIECES, TILE, WIDE), jnp.float32)

    def fill_places():
        place = (target_col - owner_col * rows + 1).astype(jnp.float32)
        lane = iota((rows, slots), 1)
        here = lane == me * capacity + rank_col
        seam_row = seam[...]
        seam_col = upright(jnp.where(seam_row >= 0, seam_row + 1, -1)).astype(jnp.float32)
        seam_line = jnp.sum(jnp.where(lane == iota((rows, slots), 0), seam_col, 0.0), axis=0, keepdims=True)
        for dest in range(peers):
            line = jnp.sum(
                jnp.where(here & (owner_col == dest), place, 0.0), axis=0, keepdims=True
            )
            place_send[dest] = jnp.where(iota((TILE, slots), 0) == 0, line, seam_line)

    first_tile, final_tile = pl.ds(TILE, TILE), pl.ds(rows, TILE)
    above_tile, below_tile = pl.ds(0, TILE), pl.ds(TILE + rows, TILE)

    def send_slots(piece):
        settle(held.at[piece], load_sems.at[piece])
        if piece + 1 < PIECES:
            load_piece(piece + 1)
        looks = form_piece(piece, held, group, hold)
        slot_send[piece] = pick_dot(choose, looks).reshape(peers, capacity, WIDE)
        if piece == 0:
            pl.semaphore_wait(barrier, peers)
        for offset in range(peers - 1, 0, -1):
            send(
                slot_send.at[piece, facing(offset)],
                slot_recv.at[piece, me],
                at(facing(offset), core),
                slot_send_sem,
                slot_sems.at[piece],
            )
        slot_recv[piece, me] = slot_send[piece, me]
        if piece == 0:
            fill_places()
            for offset in range(peers - 1, 0, -1):
                send(
                    place_send.at[facing(offset)],
                    place_recv.at[me],
                    at(facing(offset), core),
                    place_sems.at[0],
                    place_sems.at[1],
                )
            place_recv[me] = place_send[me]

    for piece in range(PIECES):
        send_slots(piece)
    for load in table_loads:
        load.start()

    @pl.when(me > 0)
    def _():
        send(
            weight.at[first_tile, own_lanes],
            weight.at[below_tile, own_lanes],
            at(behind(1), core),
            edge_sems.at[0],
            edge_sems.at[1],
        )

    @pl.when(me < last)
    def _():
        send(
            weight.at[final_tile, own_lanes],
            weight.at[above_tile, own_lanes],
            at(ahead(1), core),
            edge_sems.at[2],
            edge_sems.at[3],
        )

    settle(place_recv.at[pl.ds(0, last)], place_sems.at[1])
    places = place_recv[0][0:1]
    for source in range(1, peers):
        places = places + place_recv[source][0:1]
    seam_wanted = upright(place_recv[behind(1)][1:2, :rows])
    own_wanted = (iota((rows, slots), 0) + 1).astype(jnp.float32)
    scatter = jnp.concatenate(
        [
            jnp.where(places == seam_wanted, 1.0, 0.0),
            jnp.where(places == own_wanted, 1.0, 0.0),
        ],
        axis=0,
    ).astype(jnp.bfloat16)
    scatter = jnp.concatenate([scatter] * 3, axis=1)

    @pl.when(me < last)
    def _():
        settle(weight.at[below_tile, own_lanes], edge_sems.at[1])

    @pl.when(me > 0)
    def _():
        settle(weight.at[above_tile, own_lanes], edge_sems.at[3])

    send(
        weight.at[:, own_lanes],
        weight.at[:, own_lanes],
        at(me, other),
        edge_sems.at[4],
        edge_sems.at[5],
    )
    head = pl.ds(0, rows + TILE)
    top = pl.ds(0, TILE)
    tail = pl.ds(2 * rows - TILE, TILE)

    def send_seams(piece):
        settle(slot_recv.at[piece, pl.ds(0, last)], slot_sems.at[piece])
        arrived = slot_recv[piece].reshape(slots, WIDE)
        grid_out[piece] = pick_dot(scatter, arrived)

        @pl.when(me > 0)
        def _():
            send(
                grid_out.at[piece, head],
                seam_recv.at[piece, after],
                at(behind(1), core),
                seam_send_sems.at[0],
                seam_sems.at[piece],
            )

        @pl.when(me > 1)
        def _():
            send(
                grid_out.at[piece, top],
                seam_recv.at[piece, beyond],
                at(behind(2), core),
                seam_send_sems.at[1],
                seam_sems.at[piece],
            )

        @pl.when(me < last)
        def _():
            send(
                grid_out.at[piece, tail],
                seam_recv.at[piece, before],
                at(ahead(1), core),
                seam_send_sems.at[2],
                seam_sems.at[piece],
            )

    part_of = iota((ends, LANES), 1) // PART

    def send_gamma(piece, planes):
        @pl.when((me > 0) & (me < last - 1))
        def _():
            settle(seam_recv.at[piece], seam_sems.at[piece])

        @pl.when((me == 0) | (me == last - 1))
        def _():
            settle(seam_recv.at[piece, pl.ds(0, ends)], seam_sems.at[piece])

        @pl.when(me == last)
        def _():
            settle(seam_recv.at[piece, before], seam_sems.at[piece])

        own = grid_out[piece]
        coming = seam_recv[piece]
        combined = jnp.concatenate(
            [
                coming[ends:] + own[rows - TILE : rows],
                own[rows:] + coming[:rows],
                coming[rows : rows + TILE] + coming[rows + TILE : ends],
            ],
            axis=0,
        )
        powers = combined[:, LANES:]
        gamma = combined[:, :LANES] / (jnp.sqrt(powers * pltpu.roll(powers, PART, 1)) + EPSILON)
        tile, spot = piece * PART // LANES, piece % (LANES // PART)
        for plane in range(2):
            moved = (spot - plane) * PART % LANES
            part = pltpu.roll(gamma, moved, 1) if moved else gamma
            planes[plane] = jnp.where(part_of == spot, part, planes[plane]) if spot else part
        if spot == LANES // PART - 1:
            place = core * (cols // LANES) + tile
            for plane in range(2):
                fields[plane, place] = planes[plane]
            send(
                fields.at[:, place],
                fields.at[:, place],
                at(me, other),
                gamma_send_sem,
                gamma_sems.at[tile],
            )

    planes = [None, None]
    for piece in range(PIECES + LAG):
        if piece < PIECES:
            send_seams(piece)
        if piece >= LAG:
            send_gamma(piece - LAG, planes)
    for load in table_loads:
        load.wait()
    settle(weight.at[:, own_lanes], edge_sems.at[5])

    column = iota((rows, length), 1)

    def beside(values):
        middle = values[TILE : TILE + rows]
        return (
            values[TILE - 1 : TILE - 1 + rows],
            values[TILE + 1 : TILE + 1 + rows],
            pltpu.roll(middle, 1, 1),
            pltpu.roll(middle, length - 1, 1),
        )

    weights = weight[...]
    inside = weights[TILE : TILE + rows]
    edges = [inside * item for item in beside(weights)]
    edges[2] = jnp.where(column > 0, edges[2], 0.0)
    edges[3] = jnp.where(column < length - 1, edges[3], 0.0)
    tiles = cols // LANES
    for tile in range(tiles):
        settle(fields.at[:, tile], gamma_sems.at[tile])
    real, imag = [
        jnp.concatenate([fields[plane, tile] for tile in range(2 * tiles)], axis=1)
        for plane in range(2)
    ]
    right_side = jnp.zeros((rows, length), jnp.float32)
    for edge, real_item, imag_item in zip(edges, beside(real), beside(imag)):
        right_side = right_side + edge * (
            imag[TILE : TILE + rows] * real_item - real[TILE : TILE + rows] * imag_item
        )

    def operator(values):
        middle = values[TILE : TILE + rows]
        result = damping * middle
        for edge, item in zip(edges, beside(values)):
            result = result + edge * (middle - item)
        return result

    def fold(values):
        total = None
        for row in range(0, rows, TILE):
            for begin in range(0, length, LANES):
                part = values[row : row + TILE, begin : begin + LANES]
                total = part if total is None else total + part
        return total

    def share(turn, tiles):
        for index, tile in enumerate(tiles):
            note_send[turn, index * TILE : (index + 1) * TILE] = tile
        used = pl.ds(0, len(tiles) * TILE)
        for offset in range(peers - 1, 0, -1):
            send(
                note_send.at[turn, used],
                note_recv.at[turn, me, used],
                at(facing(offset), core),
                note_sems.at[turn, 0],
                note_sems.at[turn, 1],
            )
        note_recv[turn, me, used] = note_send[turn, used]
        return used

    def collect(turn, used):
        settle(note_recv.at[turn, pl.ds(0, last), used], note_sems.at[turn, 1])

    def totals(turn, first, count):
        results = []
        for index in range(first, first + count):
            total = note_recv[turn, 0, index * TILE : (index + 1) * TILE]
            for source in range(1, peers):
                total = total + note_recv[turn, source, index * TILE : (index + 1) * TILE]
            results.append(jnp.sum(total, keepdims=True))
        return results

    forward_parts = [forward[part] for part in range(3)]
    inverse_parts = [inverse[part] for part in range(3)]
    quarter = length // LANES

    def as_row(tile):
        return jnp.concatenate([tile[index : index + 1] for index in range(quarter)], axis=1)

    def precondition(turn, values, products):
        spectrum = basis_dot(values, forward_parts)
        from_top, from_end, inverted = table[0], table[1], table[2]
        first = jnp.sum(spectrum * from_top, axis=0, keepdims=True)
        final = jnp.sum(spectrum * from_end, axis=0, keepdims=True)
        rims = jnp.concatenate(
            [
                line[:, begin : begin + LANES]
                for line in (first, final)
                for begin in range(0, length, LANES)
            ],
            axis=0,
        )
        used = share(turn, [rims] + [fold(product) for product in products])
        alone = left_dot(local[1], left_dot(local[0], spectrum) * inverted)
        collect(turn, used)
        jumps = []
        for which in range(2):
            total = couple[which, 0] * note_recv[turn, 0, 0:TILE]
            for source in range(1, peers):
                total = total + couple[which, source] * note_recv[turn, source, 0:TILE]
            jumps.append(as_row(total[:quarter] + total[quarter:]))
        below, above = jumps
        solved = alone - from_end * below + from_top * above
        padded = jnp.concatenate(
            [
                jnp.broadcast_to(solved[0:1] + above, (TILE, length)),
                solved,
                jnp.broadcast_to(solved[rows - 1 :] - below, (TILE, length)),
            ],
            axis=0,
        )
        return basis_dot(padded, inverse_parts)

    z0 = precondition(0, right_side, [])
    z0_mid = z0[TILE : TILE + rows]
    w0 = operator(z0)
    y0 = precondition(1, w0, [right_side * z0_mid, z0_mid * w0])
    rho0, energy0 = totals(1, 1, 2)
    alpha0 = rho0 / energy0
    r1 = right_side - alpha0 * w0
    z1 = z0 - alpha0 * y0
    z1_mid = z1[TILE : TILE + rows]
    q1 = operator(z1)
    collect(2, share(2, [fold(r1 * z1_mid), fold(z1_mid * q1), fold(z0_mid * q1)]))
    rho1, energy1, cross = totals(2, 0, 3)
    beta = rho1 / rho0
    alpha1 = rho1 / (energy1 + 2.0 * beta * cross + beta * beta * energy0)
    answer = alpha0 * z0_mid + alpha1 * (z1_mid + beta * z0_mid)
    left = r1 - alpha1 * (q1 + beta * w0)
    out_ref[0] = jnp.where(core == 0, answer[:, :cols], answer[:, cols:])
    out_ref[1] = jnp.where(core == 0, left[:, :cols], left[:, cols:])

    settle(place_send.at[pl.ds(0, last)], place_sems.at[0])
    settle(slot_send.at[:, pl.ds(0, last)], slot_send_sem)
    settle(weight.at[:, own_lanes], edge_sems.at[4])
    settle(fields.at[:, pl.ds(0, tiles)], gamma_send_sem)
    settle(note_recv.at[0, pl.ds(0, last), top], note_sems.at[0, 0])
    settle(note_recv.at[1, pl.ds(0, last)], note_sems.at[1, 0])
    settle(note_recv.at[2, pl.ds(0, last)], note_sems.at[2, 0])

    @pl.when(me > 0)
    def _():
        settle(weight.at[first_tile, own_lanes], edge_sems.at[0])
        settle(grid_out.at[:, head], seam_send_sems.at[0])

    @pl.when(me > 1)
    def _():
        settle(grid_out.at[:, top], seam_send_sems.at[1])

    @pl.when(me < last)
    def _():
        settle(weight.at[final_tile, own_lanes], edge_sems.at[2])
        settle(grid_out.at[:, tail], seam_send_sems.at[2])


def fits_kernel(peers, cores, rows, cols):
    length = rows * peers
    capacity = max(2, 2 * rows // peers)
    return (
        cores == 2
        and rows == 64
        and length == cols * cores
        and length == 4 * LANES
        and peers * capacity == LANES
        and peers == TILE
    )


def dct_matrix(length):
    freq = np.arange(length)
    angle = (2 * freq[None, :] + 1) * freq[:, None] % (4 * length)
    scale = np.sqrt(np.where(freq == 0, 1.0, 2.0) / length)
    return scale[:, None] * np.cos(angle * (math.pi / (2.0 * length)))


def exact_eigenvalues(length):
    return 4.0 * np.sin(np.arange(length) * (math.pi / (2.0 * length))) ** 2


def bf16_parts(matrix):
    parts, rest = [], matrix
    for _ in range(3):
        parts.append(rest.astype(jnp.bfloat16))
        rest = rest - parts[-1].astype(np.float64)
    return parts


def left_parts(matrix):
    first, second, third = bf16_parts(matrix)
    return np.concatenate([first, second, third, first, second, first], axis=1)


def solve_tables(peers, rows, length, damping):
    small = dct_matrix(rows)
    shift = exact_eigenvalues(length) + damping
    inverted = 1.0 / (exact_eigenvalues(rows)[:, None] + shift[None, :])
    from_top = small.T @ (small[:, 0:1] * inverted)
    near, far = from_top[0], from_top[-1]
    count = peers - 1
    system = np.zeros((length, count, count))
    for index in range(count):
        system[:, index, index] = 1.0 + 2.0 * near
        if index:
            system[:, index, index - 1] = -far
            system[:, index - 1, index] = -far
    solved = np.linalg.inv(system)
    couple = np.zeros((peers, peers, 2, length))
    for jump in range(count):
        for index in range(count):
            couple[jump, index, 1] += solved[:, jump, index]
            couple[jump, index + 1, 0] -= solved[:, jump, index]
    tables = np.stack([from_top, from_top[::-1], inverted]).astype(np.float32)
    couple = couple.reshape(peers, peers, 2 * length // LANES, LANES).astype(np.float32)
    return np.stack([left_parts(small), left_parts(small.T)]), tables, couple


def unwrap_in_kernel(reference_slc, secondary_slc, line_target, seam_partner, mask_level, peers):
    rows, cols = mask_level.shape
    length = rows * peers
    capacity = max(2, 2 * rows // peers)
    slots = peers * capacity
    damping = 0.25 / (rows * rows)
    basis = dct_matrix(length)
    inverse = np.stack(bf16_parts(basis))
    forward = np.stack(bf16_parts(basis.T))
    local, tables, couple = solve_tables(peers, rows, length, damping)
    width = reference_slc.shape[2] // PIECES
    lines = reference_slc.shape[1]
    group = (np.arange(width)[:, None] // LOOK_RG == np.arange(LANES)[None, :]).astype(jnp.bfloat16)
    hbm = pl.BlockSpec(memory_space=pl.ANY)
    vmem = pl.BlockSpec(memory_space=pltpu.VMEM)
    dma = pltpu.SemaphoreType.DMA

    def scratch(*dims):
        return pltpu.VMEM(dims, jnp.float32)

    def like(array):
        return pltpu.VMEM(array.shape, array.dtype)

    target, seam = line_target.reshape(1, rows), seam_partner.reshape(1, rows)
    both = pl.pallas_call(
        functools.partial(unwrap_kernel, peers, capacity, damping),
        out_shape=pltpu.VMEM((2, rows, cols), jnp.float32),
        in_specs=[hbm] * 11,
        out_specs=vmem,
        scratch_shapes=[
            pltpu.VMEM((PIECES, 2, 2, lines, width), jnp.bfloat16),
            like(group),
            like(target),
            like(seam),
            like(mask_level),
            like(forward),
            like(inverse),
            like(local),
            like(tables),
            scratch(2, peers, TILE, LANES),
            scratch(width // LANES * (lines // LINES), 4 * LINES, LANES),
            scratch(peers, TILE, slots),
            scratch(peers, TILE, slots),
            scratch(PIECES, peers, capacity, WIDE),
            scratch(PIECES, peers, capacity, WIDE),
            scratch(PIECES, 2 * rows, WIDE),
            scratch(PIECES, rows + 3 * TILE, WIDE),
            scratch(rows + 2 * TILE, length),
            scratch(2, length // LANES, rows + 2 * TILE, LANES),
            scratch(3, 3 * TILE, LANES),
            scratch(3, peers, 3 * TILE, LANES),
            dma((PIECES,)),
            dma((10,)),
            dma((2,)),
            dma,
            dma((PIECES,)),
            dma((3,)),
            dma((PIECES,)),
            dma((6,)),
            dma,
            dma((cols // LANES,)),
            dma((3, 2)),
        ],
        compiler_params=pltpu.CompilerParams(
            collective_id=0, has_side_effects=True, vmem_limit_bytes=63 * 2**20
        ),
        name="unwrap",
    )(
        reference_slc,
        secondary_slc,
        group,
        target,
        seam,
        mask_level,
        forward,
        inverse,
        local,
        tables,
        couple,
    )
    return both[0], both[1]


def pick_rows(wanted, stack):
    choose = (wanted[:, None] == jnp.arange(stack.shape[1], dtype=jnp.int32)).astype(jnp.float32)
    return jnp.einsum("sr,prc->psc", choose, stack, precision=FULL_PRECISION)


def single_product(left, right):
    return lax.psum(jnp.sum(left * right), ("az", "rg"))


def on_device(reference_slc, secondary_slc, line_target, seam_partner, mask_level):
    dev_count = lax.axis_size("az")
    rg_count = lax.axis_size("rg")
    az_place = lax.axis_index("az")
    rg_place = lax.axis_index("rg")
    row_count = line_target.shape[0]
    col_count = mask_level.shape[1]
    if fits_kernel(dev_count, rg_count, row_count, col_count):
        return unwrap_in_kernel(
            reference_slc, secondary_slc, line_target, seam_partner, mask_level, dev_count
        )
    local_sums = form_looks(reference_slc, secondary_slc, col_count)
    capacity = max(2, 2 * row_count // dev_count)
    owners = line_target // row_count
    local_index = jnp.arange(row_count, dtype=jnp.int32)
    earlier = (owners[:, None] == owners[None, :]) & (local_index[None, :] < local_index[:, None])
    slot_rank = jnp.sum(earlier.astype(jnp.int32), axis=1)
    slot_index = owners * capacity + slot_rank
    buffer_length = dev_count * capacity
    source_row = jnp.full((buffer_length,), row_count, jnp.int32).at[slot_index].set(local_index)
    positions = (
        jnp.full((1, buffer_length), row_count, jnp.int32)
        .at[0, slot_index]
        .set(line_target % row_count)
    )
    sent_sums = pick_rows(source_row, local_sums)
    got_sums, got_positions = (
        lax.all_to_all(sent_sums, "az", split_axis=1, concat_axis=1, tiled=True),
        lax.all_to_all(positions, "az", split_axis=1, concat_axis=1, tiled=True),
    )
    gridded = jnp.zeros_like(local_sums).at[:, got_positions[0]].set(got_sums, mode="drop")
    next_block = from_behind(gridded, "az", -1)
    combined = gridded + pick_rows(seam_partner, next_block)
    magnitude = jnp.sqrt(combined[2] * combined[3]) + EPSILON
    weight = (1 + mask_level).astype(jnp.float32) * 0.25
    fields = jnp.stack([combined[0] / magnitude, combined[1] / magnitude, weight])
    padded = with_halo(fields, (("az", 1), ("rg", 2)), 1)
    beside_all = neighbours(padded)
    edge_weights = [weight * item[2] for item in beside_all]
    right_side = jnp.zeros((row_count, col_count), jnp.float32)
    for edge, item in zip(edge_weights, beside_all):
        right_side = right_side + edge * (fields[1] * item[0] - fields[0] * item[1])
    damping = 0.25 / (row_count * row_count)
    grid_rows = row_count * dev_count
    grid_cols = col_count * rg_count
    my_cols = rg_place * col_count + jnp.arange(col_count, dtype=jnp.int32)
    column_width = col_count // dev_count
    all_rows = jnp.arange(grid_rows, dtype=jnp.int32)
    full_basis = dct_table(all_rows, all_rows, grid_rows)
    pencil_cols = (
        rg_place * col_count + az_place * column_width + jnp.arange(column_width, dtype=jnp.int32)
    )
    pencil_divisor = (
        eigenvalues(pencil_cols, grid_cols)[:, None]
        + eigenvalues(all_rows, grid_rows)[None, :]
        + damping
    )

    def precondition(values):
        basis_block = dct_table(
            jnp.arange(col_count * lax.axis_size("rg"), dtype=jnp.int32), my_cols, grid_cols
        )
        range_spectrum = lax.psum_scatter(
            contract(basis_block, values, 1, 1), "rg", scatter_dimension=0, tiled=True
        )
        pencil = lax.all_to_all(range_spectrum, "az", split_axis=0, concat_axis=1, tiled=True)
        filtered = contract(pencil, full_basis, 1, 1) / pencil_divisor
        restored = contract(filtered, full_basis, 1, 0)
        back_columns = lax.all_to_all(restored, "az", split_axis=1, concat_axis=0, tiled=True)
        basis_block = dct_table(
            my_cols, jnp.arange(col_count * lax.axis_size("rg"), dtype=jnp.int32), grid_cols
        )
        return lax.psum_scatter(
            contract(basis_block, back_columns, 0, 0), "rg", scatter_dimension=0, tiled=True
        ).T

    solution = jnp.zeros((row_count, col_count), jnp.float32)
    residual = right_side
    precond = precondition(residual)
    direction = precond
    inner_now = single_product(residual, precond)
    for turn_index in range(ITERS):
        rim = with_halo(direction, (("az", 0), ("rg", 1)), 1)
        result_sum = damping * direction
        for apply_edge, apply_item in zip(edge_weights, neighbours(rim)):
            result_sum = result_sum + apply_edge * (direction - apply_item)
        step_size = inner_now / lax.psum(jnp.sum(direction * result_sum), ("az", "rg"))
        solution = solution + step_size * direction
        residual = residual - step_size * result_sum
        if turn_index + 1 < ITERS:
            precond = precondition(residual)
            inner_next = single_product(residual, precond)
            direction = precond + inner_next / inner_now * direction
            inner_now = inner_next
    return (solution, residual)


def solution(mesh):
    in_specs = (
        P(None, ("pass", "az"), "rg"),
        P(None, ("pass", "az"), "rg"),
        P(("pass", "az")),
        P(("pass", "az")),
        P(("pass", "az"), "rg"),
    )
    out_specs = (P(("pass", "az"), "rg"), P(("pass", "az"), "rg"))
    return jax.shard_map(
        on_device, mesh=mesh, in_specs=in_specs, out_specs=out_specs, check_vma=False
    )
```
